512 devices in a mesh: ent: 128 (over y, z, core), rep: 4 (over x).
Axes of the slice: x: 4, y: 8, z: 8, core: 2. Of those that a mesh axis runs over, the one named last changes fastest.
Arguments:
- entity_table: float32 [65536, 200], P('ent'), may hold values from -6 to 6
- relation_table: bfloat16 [822, 200], replicated, may hold values from -12 to 12
- filters: float32 [32, 9], replicated, may hold values from -2 to 2
- projection: bfloat16 [9728, 200], replicated, may hold values from -0.0625 to 0.0625
- request_owner: int32 [163840, 1], P(('ent', 'rep')), may hold values from 0 to 127; in each aligned block of 320 rows (0 to 319, 320 to 639, ...) at most 4 rows name the same one
- request_row: int32 [163840], P(('ent', 'rep')), may hold values from 0 to 511
- relation_id: int32 [65536], P(('ent', 'rep')), may hold values from 0 to 821
- rare_flag: int32 [65536], P('ent'), may hold values 0 or 1
- running_norm: float32 [], replicated, may hold values from 2 to 6
Outputs:
- new_table: float32 [65536, 200], P('ent')
- filter_grad: float32 [32, 9], replicated
The draws below stay inside these ranges and needn't reach their ends.
Inputs may be any that keep to these rules, and one draw needn't show every extreme that they name: `request_owner`: among the requests of one device no owner shard is named more than 4 times, a bound that some block reaches.
All inputs are finite; a program needn't handle non-finite values. No bound on the sum of `rare_flag` on one device may be relied on, other than what follows from the above.
Results may differ from the reference program's by a relative error of at most 0.002.
Values sent between devices are 32-bit elements; how exact they have to be, the bound alone decides.
A program may use at most 64 MiB of HBM per device.

```python
import math
import jax
import jax.numpy as jnp
import numpy as np
from jax import lax

D = 200
ROWS = 20
FILT = 32
FEAT = 9728
RELS = 822
ENT_DEV = 512
REQ = 320
CAP = 4
ENTITIES = 65536
BATCH = 65536
N_ENT = 128
N_REP = 4


def draw_entity_table(key, part):
    total_rows = ENT_DEV * N_ENT
    shard_pos = jnp.arange(N_ENT).astype(jnp.float32)
    rising = 0.25 * jnp.power(3.0, shard_pos / max(N_ENT - 1, 1))
    first_key = jax.random.fold_in(jax.random.fold_in(key, 11), 0)
    third_key = jax.random.fold_in(jax.random.fold_in(key, 11), 2)
    fourth_key = jax.random.fold_in(jax.random.fold_in(key, 11), 3)
    column_scale = jnp.exp(jax.random.uniform(third_key, (1, D), jnp.float32, -2.3026, 0.0))
    shard_factor = jnp.exp(jax.random.uniform(fourth_key, (N_ENT,), jnp.float32, -3.2, 0.95))
    values = jnp.clip(jax.random.normal(first_key, (total_rows, D), jnp.float32), -3.0, 3.0)
    per_row = jnp.repeat(rising * shard_factor, ENT_DEV, total_repeat_length=total_rows)
    scaled = values * column_scale * per_row[:, None]
    return jnp.clip(scaled, -6.0, 6.0).astype(jnp.float32)


def place_ends(drawn, stream_key, smallest, largest):
    index_at = [jax.random.randint(jax.random.fold_in(stream_key, axis), (), 0, length) for axis, length in enumerate(drawn.shape)]
    widest = drawn.shape.index(max(drawn.shape))
    neighbour = index_at[:widest] + [(index_at[widest] + 1) % drawn.shape[widest]] + index_at[widest + 1:]
    return drawn.at[tuple(index_at)].set(smallest).at[tuple(neighbour)].set(largest)


def rank_bounds(amount, slope):
    weights = [(1 << 20) // math.isqrt(grade ** slope) + 1 for grade in range(1, amount + 1)]
    deviation = 1 + sum(weights) // (1 << 30)
    return np.cumsum(np.array([max(1, weight // deviation) for weight in weights]))


def skewed_ids(rng, extent, number_of, skew):
    table = rank_bounds(number_of, skew)
    pick = jax.random.randint(jax.random.fold_in(rng, 1), extent, 0, int(table[number_of - 1]))
    grade = jnp.searchsorted(jnp.asarray(table, jnp.int32), pick, side="right")
    return jax.random.permutation(jax.random.fold_in(rng, 2), number_of)[grade].astype(jnp.int32)


def routed_block(rng, own, number, rows, count, top, reach, skew):
    sequence = jax.random.permutation(rng, count)
    heavy_load, common = shares(count, rows * top, reach, skew, True), shares(count, rows * top, reach, skew, False)
    places = jnp.arange(count)

    def named(lengths, offset_by):
        used = int((lengths > 0).sum())
        fixed = max(1, used // 4)
        passed = fixed + (places - fixed + offset_by * (used - fixed)) % max(1, count - fixed)
        return jnp.zeros((count,), jnp.int32).at[sequence[jnp.where(places < fixed, places, passed)]].set(jnp.asarray(lengths, jnp.int32))

    lengths = jnp.where(number % 4 == 0, named(heavy_load, number // 4), named(common, number - number // 4 - 1))
    mixed = jax.random.permutation(jax.random.fold_in(own, 3), count)
    source_of, receiver = mixed[0:count // 2 * 2:2], mixed[1:count // 2 * 2:2]
    margin = jnp.minimum(lengths[source_of] - 1, reach - lengths[receiver]) // 2
    margin = jnp.where((source_of == sequence[0]) | (receiver == sequence[0]) | (lengths[receiver] == 0), 0, jnp.maximum(margin, 0))
    passed = jax.random.randint(jax.random.fold_in(own, 4), (count // 2,), 0, 1 << 20) % (margin + 1)
    lengths = lengths.at[source_of].add(-passed).at[receiver].add(passed)
    labels = jnp.searchsorted(jnp.cumsum(lengths), jnp.arange(rows * top), side="right").astype(jnp.int32)
    table = labels.reshape(top, rows).T
    table = table[jax.random.permutation(jax.random.fold_in(own, 1), rows)]
    offset_by = jax.random.randint(jax.random.fold_in(own, 2), (rows, 1), 0, top)
    return jnp.take_along_axis(table, (jnp.arange(top)[None, :] + offset_by) % top, axis=1)


def shares(number_of, total, limit, slope, full):
    portions = [(1 << 20) // math.isqrt(grade ** slope) + 1 for grade in range(1, number_of + 1)]
    largest = limit if full else min(limit, max(-(-total // number_of), total * portions[0] // sum(portions)))
    least = 1 if total - largest >= number_of - 1 else 0
    holding, surplus = [largest] + [least] * (number_of - 1), total - largest - least * (number_of - 1)
    while surplus > 0:
        movable = [i for i in range(1, number_of) if holding[i] < largest] or [i for i in range(1, number_of) if holding[i] < limit]
        whole, left = sum([portions[i] for i in movable]), surplus
        for i in movable:
            more = min(limit - holding[i], max(1, left * portions[i] // whole), surplus)
            holding[i] = holding[i] + more
            surplus = surplus - more
    return np.array(holding)


def normal_values(own_key, shape, spread, most, held_as=jnp.bfloat16):
    entries = jax.random.normal(own_key, shape, jnp.float32) * spread
    return jnp.minimum(jnp.maximum(entries, -most), most).astype(held_as)


def setup_inputs(seed: int = 0) -> dict:
    splits = jax.random.split(jax.random.key(seed), 10)
    entity_table = draw_entity_table(jax.random.fold_in(splits[9], 71), 0)
    relation_table = normal_values(splits[1], (RELS, D), 3.0, 12.0)
    filters = normal_values(splits[2], (FILT, 9), 9 ** -0.5, 2.0, jnp.float32)
    projection = normal_values(splits[3], (FEAT, D), FEAT ** -0.5, 0.0625)
    request_owner_keys = jax.random.split(jax.random.fold_in(splits[4], 1), (N_ENT * N_REP * REQ) // REQ)
    request_owner_turns = jax.random.permutation(jax.random.fold_in(splits[4], 3), (N_ENT * N_REP * REQ) // REQ)
    request_owner = jax.vmap(lambda own, number: routed_block(jax.random.fold_in(splits[4], 2), own, number, REQ, N_ENT, 1, CAP, 2))(request_owner_keys, request_owner_turns).reshape((N_ENT * N_REP * REQ, 1))
    request_row = place_ends(skewed_ids(splits[5], (N_ENT * N_REP * REQ,), ENT_DEV, 2), jax.random.fold_in(splits[5], 3), 0, ENT_DEV - 1).astype(jnp.int32)
    relation_id = place_ends(jax.random.randint(splits[6], (BATCH,), 0, RELS), jax.random.fold_in(splits[6], 1), 0, RELS - 1).astype(jnp.int32)
    rare_flag = place_ends((jax.random.randint(splits[7], (ENTITIES,), 0, 4) < 1).astype(jnp.int32), jax.random.fold_in(splits[7], 1), 0, 1)
    running_norm = jnp.clip(jax.random.uniform(splits[8], (), jnp.float32, 2.0, 6.0), 2.0, 6.0)
    return dict(entity_table=entity_table, relation_table=relation_table, filters=filters, projection=projection, request_owner=request_owner, request_row=request_row, relation_id=relation_id, rare_flag=rare_flag, running_norm=running_norm)


learn_rate = 0.5
norm_eps = 1e-06

def conv_act(head_rows, rel_rows, filters):
    count = head_rows.shape[0]
    stacked = jnp.concatenate([head_rows.reshape(count, ROWS, D // ROWS), rel_rows.reshape(count, ROWS, D // ROWS)], axis=1)[:, None]
    kernel = filters.reshape(filters.shape[0], 1, 3, 3)
    conv_out = lax.conv_general_dilated(stacked, kernel, (1, 1), 'VALID', precision=lax.Precision.HIGHEST)
    return jax.nn.silu(conv_out).reshape(count, -1)

def block_step(row_values, rel_rows, filters, projection, batch_rows, neg_count):
    head_rows = row_values[:batch_rows]
    pos_rows = row_values[batch_rows:2 * batch_rows]
    neg_rows = row_values[2 * batch_rows:]
    activated, pullback = jax.vjp(lambda head_part, filt_part: conv_act(head_part, rel_rows, filt_part), head_rows, filters)
    features = activated.astype(jnp.bfloat16)
    projected = jnp.dot(features, projection, preferred_element_type=jnp.float32)
    sig_proj = jax.nn.sigmoid(projected)
    hidden = projected * sig_proj
    score_pos = lax.optimization_barrier(jnp.sum(hidden * pos_rows, 1))
    score_neg = jnp.dot(hidden, neg_rows.T, precision=lax.Precision.HIGHEST)
    grad_pos = -jax.nn.sigmoid(-score_pos)
    grad_neg = jax.nn.sigmoid(score_neg) / neg_count
    pos_grad_rows = grad_pos[:, None] * hidden
    neg_grad_rows = jnp.dot(grad_neg.T, hidden, precision=lax.Precision.HIGHEST)
    grad_hidden = grad_pos[:, None] * pos_rows + jnp.dot(grad_neg, neg_rows, precision=lax.Precision.HIGHEST)
    grad_proj = (grad_hidden * sig_proj * (1.0 + projected * (1.0 - sig_proj))).astype(jnp.bfloat16)
    grad_feat = lax.dot_general(grad_proj, projection, (((1,), (1,)), ((), ())), preferred_element_type=jnp.float32)
    head_grad_rows, filter_part = pullback(grad_feat)
    return (jnp.concatenate([head_grad_rows, pos_grad_rows, neg_grad_rows], axis=0), filter_part)

def reference(entity_table, relation_table, filters, projection, request_owner, request_row, relation_id, rare_flag, running_norm):
    dev_count = N_ENT * N_REP
    entity_ids = (request_owner[:, 0] * ENT_DEV + request_row).astype(jnp.int32)
    req_count = entity_ids.shape[0] // dev_count
    batch_rows = relation_id.shape[0] // dev_count
    neg_count = req_count - 2 * batch_rows

    def one_block(pair):
        block_ids, block_rels = pair
        row_values = entity_table[block_ids]
        rel_rows = relation_table[block_rels].astype(jnp.float32)
        return block_step(row_values, rel_rows, filters, projection, batch_rows, neg_count)
    grads, filter_parts = lax.map(one_block, (entity_ids.reshape(dev_count, req_count), relation_id.reshape(dev_count, batch_rows)))
    summed_grad = jnp.zeros_like(entity_table).at[entity_ids].add(grads.reshape(-1, entity_table.shape[1]))
    updated = entity_table - learn_rate * summed_grad
    filter_grad = lax.optimization_barrier(jnp.sum(filter_parts, 0)) / (batch_rows * dev_count)
    row_norms = jnp.sqrt(lax.optimization_barrier(jnp.sum(updated * updated, 1)) + norm_eps)
    target = 0.25 * running_norm + 0.75 * jnp.mean(row_norms)
    new_table = jnp.where((rare_flag == 1)[:, None], updated * (target / row_norms)[:, None], updated)
    return (new_table, filter_grad)
```

```python
import functools
import jax
import jax.numpy as jnp
from jax import lax
from jax.experimental import pallas as pl
from jax.experimental.pallas import tpu as pltpu
from jax.sharding import PartitionSpec as P

MESH = pl.DeviceIdType.MESH
HI = lax.Precision.HIGHEST
F32, BF16, I32 = jnp.float32, jnp.bfloat16, jnp.int32
NT = (((1,), (1,)), ((), ()))
TN = (((0,), (0,)), ((), ()))


def iota(shape, dim):
    return lax.broadcasted_iota(I32, shape, dim)


def split(v):
    high = v.astype(BF16)
    return high, (v - high.astype(F32)).astype(BF16)


def mm(a, b, dims=(((1,), (0,)), ((), ()))):
    return lax.dot_general(a, b, dims, preferred_element_type=F32)


def slot_column(ids, ent, cap):
    slots = ent * cap
    rep = (iota((slots, ent), 0) // cap == iota((slots, ent), 1)).astype(F32)
    spread = lax.dot_general(rep, ids, (((1,), (0,)), ((), ())), precision=HI, preferred_element_type=F32)
    keep = iota((slots, 128), 0) % cap == iota((slots, 128), 1)
    return jnp.sum(jnp.where(keep, spread, 0.0), 1, keepdims=True)


def fetch_kernel(ent, cap, owner_ref, row_ref, table_ref, fetched_ref, ids_ref, slot_ref,
                 send_ids, got_ids, found, id_send, id_recv, row_send, row_recv):
    me, rep = lax.axis_index("ent"), lax.axis_index("rep")
    req = owner_ref.shape[1]
    width, rows = table_ref.shape
    barrier = pltpu.get_barrier_semaphore()

    def greet(i, c):
        pl.semaphore_signal(barrier, inc=1, device_id=((me + i) % ent, rep), device_id_type=MESH)
        return c

    lax.fori_loop(1, ent, greet, 0)
    owner = owner_ref[...]
    named = iota((ent, req), 0) == owner
    named_b = named.astype(F32).astype(BF16)
    before = (iota((req, req), 0) < iota((req, req), 1)).astype(F32).astype(BF16)
    rank = jnp.sum(jnp.where(named, mm(named_b, before), 0.0), 0, keepdims=True)
    slot_ref[...] = owner * cap + rank.astype(I32)
    marked = jnp.where(iota((128, req), 0).astype(F32) == rank, row_ref[...].astype(F32), 0.0)
    ids = lax.dot_general(named.astype(F32), marked, NT, precision=HI, preferred_element_type=F32)
    send_ids[...] = ids.reshape(ent, 1, 128)
    got_ids[pl.ds(me, 1)] = send_ids[pl.ds(me, 1)]
    pl.semaphore_wait(barrier, ent - 1)

    def send_id(i, c):
        p = (me + i) % ent
        pltpu.make_async_remote_copy(
            src_ref=send_ids.at[p], dst_ref=got_ids.at[me], send_sem=id_send, recv_sem=id_recv,
            device_id=(p, rep), device_id_type=MESH).start()
        return c

    lax.fori_loop(1, ent, send_id, 0)
    high, low = split(table_ref[...])
    others = pl.ds(0, ent - 1)
    pltpu.make_async_copy(got_ids.at[others], got_ids.at[others], id_recv).wait()
    got = got_ids[...].reshape(ent, 128)
    ids_ref[...] = got
    hot = (iota((ent * cap, rows), 1).astype(F32) == slot_column(got, ent, cap)).astype(F32).astype(BF16)
    picked = mm(hot, high, NT) + mm(hot, low, NT)
    found[...] = picked.reshape(ent, cap, width)

    def send_row(i, c):
        p = (me + i) % ent
        pltpu.make_async_remote_copy(
            src_ref=found.at[p], dst_ref=fetched_ref.at[me], send_sem=row_send, recv_sem=row_recv,
            device_id=(p, rep), device_id_type=MESH).start()
        return c

    lax.fori_loop(1, ent, send_row, 0)
    fetched_ref[pl.ds(me, 1)] = found[pl.ds(me, 1)]
    pltpu.make_async_copy(send_ids.at[others], send_ids.at[others], id_send).wait()
    pltpu.make_async_copy(found.at[others], found.at[others], row_send).wait()
    pltpu.make_async_copy(fetched_ref.at[others], fetched_ref.at[others], row_recv).wait()


def fetch(owner, row, table_t, ent, cap):
    width, rows = table_t.shape
    req = owner.shape[1]
    vmem = pl.BlockSpec(memory_space=pltpu.VMEM)
    return pl.pallas_call(
        functools.partial(fetch_kernel, ent, cap),
        out_shape=(jax.ShapeDtypeStruct((ent, cap, width), F32), jax.ShapeDtypeStruct((ent, 128), F32),
                   jax.ShapeDtypeStruct((1, req), I32)),
        in_specs=[vmem] * 3, out_specs=(vmem,) * 3,
        scratch_shapes=[pltpu.VMEM((ent, 1, 128), F32), pltpu.VMEM((ent, 1, 128), F32),
                        pltpu.VMEM((ent, cap, width), F32)] + [pltpu.SemaphoreType.DMA] * 4,
        compiler_params=pltpu.CompilerParams(collective_id=0, has_side_effects=True, vmem_limit_bytes=24 << 20),
        name="fetch",
    )(owner, row, table_t)
FILT, OUT_ROWS, OUT_COLS, IMG_ROWS, IMG_COLS, PITCH = 32, 38, 8, 40, 10, 16
HEAD_ROWS = 20


def tap_masks():
    r, k = iota((16, 64), 0), iota((16, 64), 1)
    di, dj = k // PITCH - r // OUT_COLS, k % PITCH - r % OUT_COLS
    return [((di == t // 3) & (dj == t % 3)).astype(F32) for t in range(9)]


def band_matrix(filt):
    total = jnp.zeros((FILT, 16, 64), F32)
    for t, mask in enumerate(tap_masks()):
        total = total + filt[:, t : t + 1][:, :, None] * mask[None]
    return total.reshape(FILT * 16, 64)


def fill_image(img_ref, base, value_ref, rows):
    for r in range(rows):
        img_ref[pl.ds(PITCH * (base + r), IMG_COLS), :] = value_ref[pl.ds(IMG_COLS * r, IMG_COLS), :]


def compute_kernel(fetched_ref, slot_ref, rel_ref, relid_ref, filt_ref, projt_ref, proj_ref,
                   send_ref, fgrad_ref, val, img, hi_img, lo_img, feat, dact, dimg, grads, strip):
    req, batch = slot_ref.shape[1], relid_ref.shape[1]
    slots = fetched_ref.shape[0]
    width = fetched_ref.shape[1]
    neg = req - 2 * batch
    hot = (iota((slots, req), 0) == slot_ref[...]).astype(F32).astype(BF16)
    high, low = split(fetched_ref[...])
    val[...] = mm(high, hot, TN) + mm(low, hot, TN)
    rels = rel_ref.shape[1]
    pick = (iota((rels, batch), 0) == relid_ref[...]).astype(F32).astype(BF16)
    img[...] = jnp.zeros(img.shape, F32)
    strip[...] = mm(rel_ref[...], pick)
    fill_image(img, HEAD_ROWS, strip, HEAD_ROWS)
    strip[...] = val[:, pl.ds(0, batch)]
    fill_image(img, 0, strip, HEAD_ROWS)
    h, l = split(img[...])
    hi_img[...] = h
    lo_img[...] = l
    band = band_matrix(filt_ref[...])
    bh, bl = split(band)
    lhs = jnp.concatenate([bh, bh, bl], 1)

    def conv(q, c):
        at = pl.ds(pl.multiple_of(q * 2 * PITCH, 2 * PITCH), 4 * PITCH)
        hi, lo = hi_img[at, :], lo_img[at, :]
        v = mm(lhs, jnp.concatenate([hi, lo, hi], 0))
        s = 0.5 * jnp.tanh(0.5 * v) + 0.5
        a = v * s
        out = pl.ds(pl.multiple_of(q * 16, 16), 16)
        feat[:, out, :] = a.astype(BF16).reshape(FILT, 16, batch)
        dact[:, out, :] = (s + a * (1.0 - s)).reshape(FILT, 16, batch)
        return c

    lax.fori_loop(0, OUT_ROWS // 2, conv, 0)
    projected = mm(projt_ref[...], feat[...].reshape(FILT * OUT_ROWS * OUT_COLS, batch))
    sig = 0.5 * jnp.tanh(0.5 * projected) + 0.5
    hidden = projected * sig
    pos, negs = val[:, pl.ds(batch, batch)], val[:, pl.ds(2 * batch, neg)]
    dot_hi = functools.partial(lax.dot_general, precision=HI, preferred_element_type=F32)
    score_pos = jnp.sum(hidden * pos, 0, keepdims=True)
    score_neg = dot_hi(negs, hidden, TN)
    grad_pos = -jax.nn.sigmoid(-score_pos)
    grad_neg = jax.nn.sigmoid(score_neg) / neg
    grads[:, pl.ds(batch, batch)] = grad_pos * hidden
    grads[:, pl.ds(2 * batch, neg)] = dot_hi(hidden, grad_neg, NT)
    grad_hidden = grad_pos * pos + dot_hi(negs, grad_neg, (((1,), (0,)), ((), ())))
    grad_proj = (grad_hidden * sig * (1.0 + projected * (1.0 - sig))).astype(BF16)
    dimg[...] = jnp.zeros(dimg.shape, F32)
    acc0 = jnp.zeros((FILT * 16, 128), F32)

    def back(q, acc):
        out = pl.ds(pl.multiple_of(q * 16, 16), 16)
        at = pl.ds(pl.multiple_of(q * 2 * PITCH, 2 * PITCH), 4 * PITCH)
        pr = proj_ref[:, out, :].reshape(FILT * 16, width)
        d = mm(pr, grad_proj) * dact[:, out, :].reshape(FILT * 16, batch)
        dh, dl = split(d)
        hi, lo = hi_img[at, :], lo_img[at, :]
        left = jnp.concatenate([dh, dl], 1)
        zero = jnp.zeros_like(lo)
        right = jnp.concatenate([jnp.concatenate([hi, hi], 1), jnp.concatenate([lo, zero], 1)], 0)
        acc = acc + mm(left, right, NT)

        @pl.when(q < HEAD_ROWS // 2)
        def _():
            part = mm(jnp.concatenate([bh, bl], 1), dh, TN)
            dimg[at, :] += part[:64] + part[64:] + mm(bh, dl, TN)

        return acc

    acc = lax.fori_loop(0, OUT_ROWS // 2, back, acc0)
    for r in range(HEAD_ROWS):
        strip[pl.ds(IMG_COLS * r, IMG_COLS), :] = dimg[pl.ds(PITCH * r, IMG_COLS), :]
    grads[:, pl.ds(0, batch)] = strip[...]
    joint = (acc[:, :64] + acc[:, 64:]).reshape(FILT, 16, 64)
    fgrad_ref[...] = jnp.zeros(fgrad_ref.shape, F32)
    for t, mask in enumerate(tap_masks()):
        fgrad_ref[t : t + 1, :FILT] = jnp.sum(jnp.sum(joint * mask[None], 1), 1).reshape(1, FILT)
    gh, gl = split(grads[...])
    send_ref[...] = mm(hot, gh, NT) + mm(hot, gl, NT)


def compute(fetched, slot, rel_t, relid, filt, proj_t, proj):
    slots, width = fetched.shape
    req, batch, feats = slot.shape[1], relid.shape[1], proj.shape[0]
    per = OUT_ROWS * OUT_COLS
    vmem = pl.BlockSpec(memory_space=pltpu.VMEM)
    return pl.pallas_call(
        compute_kernel,
        out_shape=(jax.ShapeDtypeStruct((slots, width), F32), jax.ShapeDtypeStruct((16, 128), F32)),
        in_specs=[vmem] * 7, out_specs=(vmem,) * 2,
        scratch_shapes=[pltpu.VMEM((width, req), F32), pltpu.VMEM((IMG_ROWS * PITCH, batch), F32),
                        pltpu.VMEM((IMG_ROWS * PITCH, batch), BF16), pltpu.VMEM((IMG_ROWS * PITCH, batch), BF16),
                        pltpu.VMEM((FILT, per, batch), BF16), pltpu.VMEM((FILT, per, batch), F32),
                        pltpu.VMEM((HEAD_ROWS * PITCH + 2 * PITCH, batch), F32), pltpu.VMEM((width, req), F32),
                        pltpu.VMEM((width, batch), F32)],
        compiler_params=pltpu.CompilerParams(vmem_limit_bytes=40 << 20),
        name="triples",
    )(fetched, slot, rel_t, relid, filt, proj_t, proj.reshape(FILT, per, width))
learn_rate, norm_eps = 0.5, 1e-06
NORM_ROW = 9


def merge_kernel(ent, reps, cap, group, grads_ref, ids_ref, table_ref, small_ref, rare_ref, run_ref,
                 out_ref, total_ref, land, part, pland, upd, s_here, s_x, s_g, s_y, row_send, row_recv,
                 part_send, part_recv, upd_send, upd_recv, sx_send, sx_recv, sg_send, sg_recv, sy_send, sy_recv):
    me, rep = lax.axis_index("ent"), lax.axis_index("rep")
    width, rows = table_ref.shape
    piece = rows // reps
    outer = ent // group
    y, g = me // group, me % group
    barrier = pltpu.get_barrier_semaphore()

    def loop(start, stop, step):
        lax.fori_loop(start, stop, lambda i, c: (step(i), c)[1], 0)

    def remote(src, dst, send, recv, p, r):
        pltpu.make_async_remote_copy(src_ref=src, dst_ref=dst, send_sem=send, recv_sem=recv,
                                     device_id=(p, r), device_id_type=MESH).start()

    def drain(ref, count, sem):
        at = ref.at[pl.ds(0, count)]
        pltpu.make_async_copy(at, at, sem).wait()

    def columns(r):
        return pl.ds(pl.multiple_of(r * piece, piece), piece)

    loop(1, ent, lambda i: pl.semaphore_signal(barrier, inc=1, device_id=((me + i) % ent, rep), device_id_type=MESH))
    loop(1, reps, lambda i: pl.semaphore_signal(barrier, inc=1, device_id=(me, (rep + i) % reps), device_id_type=MESH))
    pl.semaphore_wait(barrier, ent + reps - 2)

    def send_row(i):
        p = (me + i) % ent
        remote(grads_ref.at[p], land.at[me], row_send, row_recv, p, rep)

    loop(1, ent, send_row)
    land[pl.ds(me, 1)] = grads_ref[pl.ds(me, 1)]
    hot = (iota((ent * cap, rows), 1).astype(F32) == slot_column(ids_ref[...], ent, cap)).astype(F32).astype(BF16)
    drain(grads_ref, ent - 1, row_send)
    drain(land, ent - 1, row_recv)
    high, low = split(land[...].reshape(ent * cap, width))
    sums = mm(high, hot, TN) + mm(low, hot, TN)
    for r in range(reps):
        part[r] = sums[:, r * piece : (r + 1) * piece]
    pland[pl.ds(rep, 1)] = part[pl.ds(rep, 1)]
    loop(1, reps, lambda i: remote(part.at[(rep + i) % reps], pland.at[rep], part_send, part_recv, me, (rep + i) % reps))
    drain(part, reps - 1, part_send)
    drain(pland, reps - 1, part_recv)
    block = table_ref[:, columns(rep)] - learn_rate * jnp.sum(pland[...], 0)
    upd[:, columns(rep)] = block
    mine = upd.at[:, columns(rep)]
    norms = jnp.sqrt(jnp.sum(block * block, 0, keepdims=True) + norm_eps)
    here = jnp.where(iota((16, piece), 0) == NORM_ROW, norms, small_ref[...])
    s_here[0] = here
    s_x[pl.ds(rep, 1)] = here[None]
    loop(1, reps, lambda i: remote(s_here.at[0], s_x.at[rep], sx_send, sx_recv, me, (rep + i) % reps))
    loop(1, reps, lambda i: remote(mine, upd.at[:, columns(rep)], upd_send, upd_recv, me, (rep + i) % reps))
    drain(s_x, reps - 1, sx_recv)
    s_here[1] = jnp.sum(s_x[...], 0)
    s_g[pl.ds(g, 1)] = s_here[pl.ds(1, 1)]
    loop(1, group, lambda i: remote(s_here.at[1], s_g.at[g], sg_send, sg_recv, y * group + (g + i) % group, rep))
    drain(s_g, group - 1, sg_recv)
    s_here[2] = jnp.sum(s_g[...], 0)
    s_y[pl.ds(y, 1)] = s_here[pl.ds(2, 1)]
    loop(1, outer, lambda i: remote(s_here.at[2], s_y.at[y], sy_send, sy_recv, (y + i) % outer * group + g, rep))
    drain(s_y, outer - 1, sy_recv)
    total = jnp.sum(s_y[...], 0)
    total_ref[...] = total
    norm_total = jnp.sum(total[NORM_ROW : NORM_ROW + 1, :], 1, keepdims=True)
    target = 0.25 * run_ref[...] + 0.75 * norm_total / (rows * ent)
    drain(s_x, reps - 1, sx_send)
    drain(s_g, group - 1, sg_send)
    drain(s_y, outer - 1, sy_send)
    three = upd.at[:, pl.ds(0, (reps - 1) * piece)]
    pltpu.make_async_copy(three, three, upd_send).wait()
    pltpu.make_async_copy(three, three, upd_recv).wait()
    updated = upd[...]
    norm = jnp.sqrt(jnp.sum(updated * updated, 0, keepdims=True) + norm_eps)
    out_ref[...] = updated * jnp.where(rare_ref[...] == 1, target / norm, 1.0)


def merge(grads, ids, table_t, small, rare, run, ent, reps, cap, group):
    width, rows = table_t.shape
    piece = rows // reps
    vmem = pl.BlockSpec(memory_space=pltpu.VMEM)
    return pl.pallas_call(
        functools.partial(merge_kernel, ent, reps, cap, group),
        out_shape=(jax.ShapeDtypeStruct((width, rows), F32), jax.ShapeDtypeStruct((16, 128), F32)),
        in_specs=[vmem] * 6, out_specs=(vmem,) * 2,
        scratch_shapes=[pltpu.VMEM((ent, cap, width), F32), pltpu.VMEM((reps, width, piece), F32),
                        pltpu.VMEM((reps, width, piece), F32), pltpu.VMEM((width, rows), F32),
                        pltpu.VMEM((3, 16, 128), F32), pltpu.VMEM((reps, 16, 128), F32),
                        pltpu.VMEM((group, 16, 128), F32), pltpu.VMEM((ent // group, 16, 128), F32)]
        + [pltpu.SemaphoreType.DMA] * 12,
        compiler_params=pltpu.CompilerParams(collective_id=1, has_side_effects=True, vmem_limit_bytes=24 << 20),
        name="merge",
    )(grads, ids, table_t, small, rare, run)


def body(entity_table, relation_table, filters, projection, request_owner, request_row, relation_id, rare_flag, running_norm):
    ent, reps = lax.axis_size("ent"), lax.axis_size("rep")
    cap, group = 4, 16
    table_t = entity_table.T
    batch, req = relation_id.shape[0], request_row.shape[0]
    width = table_t.shape[0]
    fetched, ids, slot = fetch(request_owner.reshape(1, req), request_row.reshape(1, req), table_t, ent, cap)
    send, small = compute(fetched.reshape(ent * cap, width), slot, relation_table.T, relation_id.reshape(1, batch),
                          filters, projection.T, projection)
    new_t, total = merge(send.reshape(ent, cap, width), ids, table_t, small, rare_flag.reshape(1, -1),
                         running_norm.reshape(1, 1), ent, reps, cap, group)
    filter_grad = total[:9, :FILT].T / (batch * ent * reps)
    return new_t.T, filter_grad


def solution(mesh):
    in_specs = (P("ent", None), P(), P(), P(), P(("ent", "rep"), None), P(("ent", "rep")), P(("ent", "rep")), P("ent"), P())
    return jax.shard_map(body, mesh=mesh, in_specs=in_specs, out_specs=(P("ent", None), P()), check_vma=False)
```

```python
import functools
import jax
import jax.numpy as jnp
from jax import lax
from jax.experimental import pallas as pl
from jax.experimental.pallas import tpu as pltpu
from jax.sharding import PartitionSpec as P

MESH = pl.DeviceIdType.MESH
HI = lax.Precision.HIGHEST
F32, BF16, I32 = jnp.float32, jnp.bfloat16, jnp.int32
NN = (((1,), (0,)), ((), ()))
NT = (((1,), (1,)), ((), ()))
TN = (((0,), (0,)), ((), ()))
learn_rate, norm_eps = 0.5, 1e-06
FILT, OUT_ROWS, OUT_COLS, IMG_ROWS, IMG_COLS, PITCH = 32, 38, 8, 40, 10, 16
HEAD_ROWS = 20
PAIRS, HEAD_PAIRS = OUT_ROWS // 2, HEAD_ROWS // 2
PER = OUT_ROWS * OUT_COLS
BAND = FILT * 16
CAP, GROUP = 4, 16
NORM_ROW = 9


def iota(shape, dim):
    return lax.broadcasted_iota(I32, shape, dim)


def mm(a, b, dims=NN):
    return lax.dot_general(a, b, dims, preferred_element_type=F32)


def mm_hi(a, b, dims=NN):
    return lax.dot_general(a, b, dims, precision=HI, preferred_element_type=F32)


def split(v):
    high = v.astype(BF16)
    return high, (v - high.astype(F32)).astype(BF16)


def one(mask):
    return mask.astype(F32).astype(BF16)


def sigmoid(v):
    return 0.5 * jnp.tanh(0.5 * v) + 0.5


def band_matrix(filt):
    r, k = iota((16, 64), 0), iota((16, 64), 1)
    di, dj = k // PITCH - r // OUT_COLS, k % PITCH - r % OUT_COLS
    total = jnp.zeros((FILT, 16, 64), F32)
    for t in range(9):
        mask = ((di == t // 3) & (dj == t % 3)).astype(F32)
        total = total + filt[:, t : t + 1][:, :, None] * mask[None]
    return total.reshape(BAND, 64)


def fill_image(img, base, strip, rows):
    for r in range(rows):
        img[pl.ds(PITCH * (base + r), IMG_COLS), :] = strip[pl.ds(IMG_COLS * r, IMG_COLS), :]


def step_kernel(ent, reps, *refs):
    (owner_h, row_h, relid_h, rare_h, run_ref, table_h, rel_h, filt_h, projt_h, out_ref, total_ref,
     owner_v, row_v, relid_v, rare_v, table_v, rel_v, filt_v, projt_v,
     proj_v, send1, got1, send2, got2, found, fetched, outgoing, land,
     val, strip, img, hi_img, lo_img, lhs_v, bandt_v, feat, dact, left_v, dimg, acc_v, turn,
     part, pland, upd, s_here, s_x, s_g, s_y, load, dma) = refs
    me, rep = lax.axis_index("ent"), lax.axis_index("rep")
    width, rows = table_v.shape
    req, batch, rels = owner_v.shape[1], relid_v.shape[0], rel_v.shape[1]
    neg = req - 2 * batch
    slots, piece, outer = ent * CAP, rows // reps, ent // GROUP
    y, g = me // GROUP, me % GROUP
    barrier = pltpu.get_barrier_semaphore()

    def loop(start, stop, step):
        lax.fori_loop(start, stop, lambda i, c: (step(i), c)[1], 0)

    def remote(src, dst, which, p, r):
        pltpu.make_async_remote_copy(src_ref=src, dst_ref=dst, send_sem=dma.at[2 * which], recv_sem=dma.at[2 * which + 1],
                                     device_id=(p, r), device_id_type=MESH).start()

    def drain(ref, count, which, side):
        at = ref.at[pl.ds(0, count)]
        pltpu.make_async_copy(at, at, dma.at[2 * which + side]).wait()

    def greet(p, r):
        pl.semaphore_signal(barrier, inc=1, device_id=(p, r), device_id_type=MESH)

    def in_group(i):
        return y * GROUP + (g + i) % GROUP

    def in_outer(i):
        return (y + i) % outer * GROUP + g

    loop(1, GROUP, lambda i: greet(in_group(i), rep))
    loop(1, outer, lambda i: greet(in_outer(i), rep))
    loop(1, reps, lambda i: greet(me, (rep + i) % reps))
    loads = [pltpu.make_async_copy(a, b, load.at[i]) for i, (a, b) in enumerate(
        [(owner_h, owner_v), (row_h, row_v), (table_h, table_v), (filt_h, filt_v), (relid_h, relid_v), (rel_h, rel_v),
         (projt_h, projt_v), (rare_h, rare_v)])]
    for copy in loads:
        copy.start()

    loads[0].wait()
    loads[1].wait()
    owner = owner_v[...]
    place = owner % GROUP * outer + owner // GROUP
    named = iota((ent, req), 0) == place
    before = one(iota((req, req), 0) < iota((req, req), 1))
    rank = jnp.sum(jnp.where(named, mm(one(named), before), 0.0), 0, keepdims=True).astype(I32)
    slot = owner * CAP + rank
    marked = jnp.where(iota((128, req), 0) == rank + g * CAP, row_v[...].reshape(1, req).astype(F32), 0.0)
    send1[...] = mm_hi(named.astype(F32), marked, NT).reshape(GROUP, outer, 128)
    got1[pl.ds(g, 1)] = send1[pl.ds(g, 1)]
    pl.semaphore_wait(barrier, GROUP + outer + reps - 3)
    loop(1, GROUP, lambda i: remote(send1.at[(g + i) % GROUP], got1.at[g], 0, in_group(i), rep))
    loads[2].wait()
    loads[3].wait()
    table_high, table_low = split(table_v[...])
    band = band_matrix(filt_v[...])
    band_high, band_low = split(band)
    lhs_v[...] = jnp.concatenate([band_high, band_high, band_low], 1)
    bandt_v[...] = jnp.concatenate([band, band - band_high.astype(F32)], 1).T.astype(BF16)
    drain(got1, GROUP - 1, 0, 1)
    send2[...] = jnp.sum(got1[...], 0).reshape(outer, 1, 128)
    got2[pl.ds(y, 1)] = send2[pl.ds(y, 1)]
    loop(1, outer, lambda i: remote(send2.at[(y + i) % outer], got2.at[y], 1, in_outer(i), rep))
    loads[4].wait()
    loads[5].wait()
    img[...] = jnp.zeros(img.shape, F32)
    strip[...] = mm(rel_v[...], one(iota((rels, batch), 0) == relid_v[...].reshape(1, batch)))
    fill_image(img, HEAD_ROWS, strip, HEAD_ROWS)
    drain(got2, outer - 1, 1, 1)
    spread = mm_hi((iota((slots, outer), 0) // (GROUP * CAP) == iota((slots, outer), 1)).astype(F32),
                   got2[...].reshape(outer, 128))
    keep = iota((slots, 128), 0) % (GROUP * CAP) == iota((slots, 128), 1)
    wanted = jnp.sum(jnp.where(keep, spread, 0.0), 1, keepdims=True)
    hot_rows = one(iota((slots, rows), 1).astype(F32) == wanted)
    picked = mm(hot_rows, table_high, NT) + mm(hot_rows, table_low, NT)
    found[...] = picked.reshape(ent, CAP, width)
    loop(1, ent, lambda i: remote(found.at[(me + i) % ent], fetched.at[me], 2, (me + i) % ent, rep))
    fetched[pl.ds(me, 1)] = found[pl.ds(me, 1)]

    loads[6].wait()

    def turn_over(i, c):
        at = pl.ds(pl.multiple_of(i * 512, 512), 512)
        proj_v[at, :] = projt_v[:, at].T
        return c

    lax.fori_loop(0, FILT * PER // 512, turn_over, 0)
    rel_at = pl.ds(HEAD_ROWS * PITCH, HEAD_ROWS * PITCH)
    hi_img[rel_at, :] = img[rel_at, :].astype(BF16)
    lo_img[rel_at, :] = jnp.zeros((HEAD_ROWS * PITCH, batch), BF16)

    def conv(q):
        at = pl.ds(pl.multiple_of(q * 2 * PITCH, 2 * PITCH), 4 * PITCH)
        hi, lo = hi_img[at, :], lo_img[at, :]
        v = mm(lhs_v[...], jnp.concatenate([hi, lo, hi], 0))
        s = sigmoid(v)
        a = v * s
        out = pl.ds(pl.multiple_of(q * 16, 16), 16)
        feat[:, out, :] = a.astype(BF16).reshape(FILT, 16, batch)
        dact[:, out, :] = (s + a * (1.0 - s)).reshape(FILT, 16, batch)

    loop(HEAD_PAIRS, PAIRS, conv)
    drain(fetched, ent - 1, 2, 1)

    hot = one(iota((slots, req), 0) == slot)
    high, low = split(fetched[...].reshape(slots, width))
    val[...] = mm(high, hot, TN) + mm(low, hot, TN)
    strip[...] = val[:, pl.ds(0, batch)]
    fill_image(img, 0, strip, HEAD_ROWS)
    head_at = pl.ds(0, HEAD_ROWS * PITCH)
    high, low = split(img[head_at, :])
    hi_img[head_at, :] = high
    lo_img[head_at, :] = low
    for q in range(HEAD_PAIRS):
        conv(q)
    projected = mm(projt_v[...], feat[...].reshape(FILT * PER, batch))
    sig = sigmoid(projected)
    hidden = projected * sig
    pos, negs = val[:, pl.ds(batch, batch)], val[:, pl.ds(2 * batch, neg)]
    score_pos = jnp.sum(hidden * pos, 0, keepdims=True)
    score_neg = mm_hi(negs, hidden, TN)
    grad_pos = -sigmoid(-score_pos)
    grad_neg = sigmoid(score_neg) / neg
    grad_hidden = grad_pos * pos + mm_hi(negs, grad_neg)
    grad_proj = (grad_hidden * sig * (1.0 + projected * (1.0 - sig))).astype(BF16)
    val[:, pl.ds(batch, batch)] = grad_pos * hidden
    val[:, pl.ds(2 * batch, neg)] = mm_hi(hidden, grad_neg, NT)
    dimg[...] = jnp.zeros(dimg.shape, F32)

    def back(q):
        out = pl.ds(pl.multiple_of(q * 16, 16), 16)
        turned = proj_v.reshape(FILT, PER, width)[:, out, :].reshape(BAND, width)
        d = mm(turned, grad_proj) * dact[:, out, :].reshape(BAND, batch)
        return split(d)

    for q in range(HEAD_PAIRS):
        dh, dl = back(q)
        left_v[q] = jnp.concatenate([dh, dl], 1)
        both = mm(bandt_v[...], dh)
        at = pl.ds(q * 2 * PITCH, 4 * PITCH)
        dimg[at, :] += both[:64] + both[64:] + mm(bandt_v[pl.ds(0, 64), :], dl)
    for r in range(HEAD_ROWS):
        strip[pl.ds(IMG_COLS * r, IMG_COLS), :] = dimg[pl.ds(PITCH * r, IMG_COLS), :]
    val[:, pl.ds(0, batch)] = strip[...]
    high, low = split(val[...])
    outgoing[...] = (mm(hot, high, NT) + mm(hot, low, NT)).reshape(ent, CAP, width)
    loop(1, ent, lambda i: remote(outgoing.at[(me + i) % ent], land.at[me], 3, (me + i) % ent, rep))
    land[pl.ds(me, 1)] = outgoing[pl.ds(me, 1)]

    acc_v[...] = jnp.zeros(acc_v.shape, F32)

    def add_filter(q, left):
        at = pl.ds(pl.multiple_of(q * 2 * PITCH, 2 * PITCH), 4 * PITCH)
        hi, lo = hi_img[at, :], lo_img[at, :]
        right = jnp.concatenate([jnp.concatenate([hi, hi], 1), jnp.concatenate([lo, jnp.zeros_like(lo)], 1)], 0)
        acc_v[...] += mm(left, right, NT)

    loop(0, HEAD_PAIRS, lambda q: add_filter(q, left_v[q]))
    loop(HEAD_PAIRS, PAIRS, lambda q: add_filter(q, jnp.concatenate(back(q), 1)))
    both = acc_v[...]
    acc_v[...] = both + pltpu.roll(both, 64, 1)
    taps = acc_v[pl.ds(0, FILT, stride=16), :]
    for k in range(1, 16):
        shift = k // OUT_COLS * PITCH + k % OUT_COLS
        taps = taps + pltpu.roll(acc_v[pl.ds(k, FILT, stride=16), :], 128 - shift, 1)
    turn[...] = jnp.concatenate([taps, jnp.zeros((128 - FILT, 128), F32)], 0).T
    filter_part = jnp.concatenate([turn[pl.ds(PITCH * i, 3), :] for i in range(3)] + [jnp.zeros((7, 128), F32)], 0)
    drain(land, ent - 1, 3, 1)

    high, low = split(land[...].reshape(slots, width))
    sums = mm(high, hot_rows, TN) + mm(low, hot_rows, TN)

    def columns(r):
        return pl.ds(pl.multiple_of(r * piece, piece), piece)

    for r in range(reps):
        part[r] = sums[:, r * piece : (r + 1) * piece]
    pland[pl.ds(rep, 1)] = part[pl.ds(rep, 1)]
    loop(1, reps, lambda i: remote(part.at[(rep + i) % reps], pland.at[rep], 4, me, (rep + i) % reps))
    drain(pland, reps - 1, 4, 1)
    block = table_v[:, columns(rep)] - learn_rate * jnp.sum(pland[...], 0)
    upd[:, columns(rep)] = block
    mine = upd.at[:, columns(rep)]
    norms = jnp.sqrt(jnp.sum(block * block, 0, keepdims=True) + norm_eps)
    here = jnp.where(iota((16, piece), 0) == NORM_ROW, norms, filter_part)
    s_here[0] = here
    s_x[pl.ds(rep, 1)] = here[None]
    loop(1, reps, lambda i: remote(s_here.at[0], s_x.at[rep], 5, me, (rep + i) % reps))
    loop(1, reps, lambda i: remote(mine, upd.at[:, columns(rep)], 8, me, (rep + i) % reps))
    drain(s_x, reps - 1, 5, 1)
    s_here[1] = jnp.sum(s_x[...], 0)
    s_g[pl.ds(g, 1)] = s_here[pl.ds(1, 1)]
    loop(1, GROUP, lambda i: remote(s_here.at[1], s_g.at[g], 6, in_group(i), rep))
    drain(s_g, GROUP - 1, 6, 1)
    s_here[2] = jnp.sum(s_g[...], 0)
    s_y[pl.ds(y, 1)] = s_here[pl.ds(2, 1)]
    loop(1, outer, lambda i: remote(s_here.at[2], s_y.at[y], 7, in_outer(i), rep))
    loads[7].wait()
    drain(send1, GROUP - 1, 0, 0)
    drain(send2, outer - 1, 1, 0)
    drain(found, ent - 1, 2, 0)
    drain(outgoing, ent - 1, 3, 0)
    drain(part, reps - 1, 4, 0)
    drain(s_x, reps - 1, 5, 0)
    drain(s_g, GROUP - 1, 6, 0)
    drain(s_y, outer - 1, 7, 1)
    drain(s_y, outer - 1, 7, 0)
    total = jnp.sum(s_y[...], 0)
    total_ref[...] = total
    norm_total = jnp.sum(total[NORM_ROW : NORM_ROW + 1, :], 1, keepdims=True)
    target = 0.25 * run_ref[...] + 0.75 * norm_total / (rows * ent)
    three = upd.at[:, pl.ds(0, (reps - 1) * piece)]
    pltpu.make_async_copy(three, three, dma.at[16]).wait()
    pltpu.make_async_copy(three, three, dma.at[17]).wait()
    updated = upd[...]
    norm = jnp.sqrt(jnp.sum(updated * updated, 0, keepdims=True) + norm_eps)
    out_ref[...] = updated * jnp.where(rare_v[...].reshape(1, rows) == 1, target / norm, 1.0)


def step(owner, row, relid, rare, run, table_t, rel_t, filt, proj_t, ent, reps):
    width, rows = table_t.shape
    req, batch, feats = owner.shape[1], relid.shape[0], proj_t.shape[1]
    piece, outer = rows // reps, ent // GROUP
    vmem, hbm = pl.BlockSpec(memory_space=pltpu.VMEM), pl.BlockSpec(memory_space=pltpu.HBM)
    v = pltpu.VMEM
    exchange = v((ent, CAP, width), F32)
    return pl.pallas_call(
        functools.partial(step_kernel, ent, reps),
        out_shape=(jax.ShapeDtypeStruct((width, rows), F32), jax.ShapeDtypeStruct((16, 128), F32)),
        in_specs=[hbm] * 4 + [vmem] + [hbm] * 4, out_specs=(vmem,) * 2,
        scratch_shapes=[
            v(owner.shape, I32), v(row.shape, I32), v(relid.shape, I32), v(rare.shape, I32), v((width, rows), F32),
            v(rel_t.shape, BF16), v(filt.shape, F32), v(proj_t.shape, BF16),
            v((feats, width), BF16), v((GROUP, outer, 128), F32), v((GROUP, outer, 128), F32), v((outer, 1, 128), F32),
            v((outer, 1, 128), F32), exchange, exchange, exchange, exchange,
            v((width, req), F32), v((width, batch), F32), v((IMG_ROWS * PITCH, batch), F32),
            v((IMG_ROWS * PITCH, batch), BF16), v((IMG_ROWS * PITCH, batch), BF16), v((BAND, 192), BF16),
            v((128, BAND), BF16), v((FILT, PER, batch), BF16), v((FILT, PER, batch), F32),
            v((HEAD_PAIRS, BAND, 2 * batch), BF16), v(((HEAD_ROWS + 2) * PITCH, batch), F32), v((BAND, 128), F32),
            v((128, 128), F32),
            v((reps, width, piece), F32), v((reps, width, piece), F32), v((width, rows), F32), v((3, 16, 128), F32),
            v((reps, 16, 128), F32), v((GROUP, 16, 128), F32), v((outer, 16, 128), F32),
            pltpu.SemaphoreType.DMA((8,)), pltpu.SemaphoreType.DMA((18,))],
        compiler_params=pltpu.CompilerParams(collective_id=0, has_side_effects=True, vmem_limit_bytes=60 << 20),
        name="step",
    )(owner, row, relid, rare, run, table_t, rel_t, filt, proj_t)


def body(entity_table, relation_table, filters, projection, request_owner, request_row, relation_id, rare_flag, running_norm):
    ent, reps = lax.axis_size("ent"), lax.axis_size("rep")
    batch, req = relation_id.shape[0], request_row.shape[0]
    new_t, total = step(request_owner.reshape(1, req), request_row, relation_id, rare_flag, running_norm.reshape(1, 1),
                        entity_table.T, relation_table.T, filters, projection.T, ent, reps)
    filter_grad = total[:9, :FILT].T / (batch * ent * reps)
    return new_t.T, filter_grad


def solution(mesh):
    in_specs = (P("ent", None), P(), P(), P(), P(("ent", "rep"), None), P(("ent", "rep")), P(("ent", "rep")), P("ent"), P())
    return jax.shard_map(body, mesh=mesh, in_specs=in_specs, out_specs=(P("ent", None), P()), check_vma=False)
```

```python
import functools
import jax
import jax.numpy as jnp
from jax import lax
from jax.experimental import pallas as pl
from jax.experimental.pallas import tpu as pltpu
from jax.sharding import PartitionSpec as P

MESH = pl.DeviceIdType.MESH
HI = lax.Precision.HIGHEST
F32, BF16, I32 = jnp.float32, jnp.bfloat16, jnp.int32
NN = (((1,), (0,)), ((), ()))
NT = (((1,), (1,)), ((), ()))
TN = (((0,), (0,)), ((), ()))
learn_rate, norm_eps = 0.5, 1e-06
FILT, OUT_ROWS, OUT_COLS, IMG_ROWS, IMG_COLS, PITCH = 32, 38, 8, 40, 10, 16
HEAD_ROWS = 20
PAIRS, HEAD_PAIRS = OUT_ROWS // 2, HEAD_ROWS // 2
PER = OUT_ROWS * OUT_COLS
BAND = FILT * 16
CAP, GROUP = 4, 16


def iota(shape, dim):
    return lax.broadcasted_iota(I32, shape, dim)


def mm(a, b, dims=NN):
    return lax.dot_general(a, b, dims, preferred_element_type=F32)


def mm_hi(a, b, dims=NN):
    return lax.dot_general(a, b, dims, precision=HI, preferred_element_type=F32)


def split(v):
    high = v.astype(BF16)
    return high, (v - high.astype(F32)).astype(BF16)


def one(mask):
    return mask.astype(F32).astype(BF16)


def sigmoid(v):
    return 0.5 * jnp.tanh(0.5 * v) + 0.5


def band_matrix(filt):
    r, k = iota((16, 64), 0), iota((16, 64), 1)
    di, dj = k // PITCH - r // OUT_COLS, k % PITCH - r % OUT_COLS
    total = jnp.zeros((FILT, 16, 64), F32)
    for t in range(9):
        mask = ((di == t // 3) & (dj == t % 3)).astype(F32)
        total = total + filt[:, t : t + 1][:, :, None] * mask[None]
    return total.reshape(BAND, 64)


def pack_tail(t, ent, tail):
    lane = iota((ent, 128), 1)
    t0, t1, t2, t3 = [t[i * ent : (i + 1) * ent] for i in range(CAP)]
    return (jnp.where(lane < tail, t0, pltpu.roll(t3, tail, 1)),
            jnp.where(lane < tail, t1, pltpu.roll(t3, 2 * tail - 128, 1)), t2)


def unpack_tail(r0, r1, r2, tail):
    lane = iota(r0.shape, 1)
    t3 = jnp.where(lane < 128 - tail, pltpu.roll(r0, 128 - tail, 1), pltpu.roll(r1, 256 - 2 * tail, 1))
    return jnp.concatenate([r0, r1, r2, t3], 0)


def fill_image(img, base, strip, rows):
    for r in range(rows):
        img[pl.ds(PITCH * (base + r), IMG_COLS), :] = strip[pl.ds(IMG_COLS * r, IMG_COLS), :]


def step_kernel(ent, reps, *refs):
    (owner_h, row_h, relid_h, rare_h, run_ref, table_h, rel_h, filt_h, projt_h, out_ref, total_ref,
     owner_v, row_v, relid_v, rare_v, table_v, rel_v, filt_v, projt_v,
     proj_v, send1, got1, send2, got2, found, fetched, out_a, out_b, land_a, land_b,
     val, strip, img, hi_img, lo_img, lhs_v, bandt_v, feat, dact, left_v, dimg, acc_v, turn,
     part_a, part_b, pland_a, pland_b, upd, f_here, f_x, f_g, f_y, n_here, n_a, n_b, load, dma) = refs
    me, rep = lax.axis_index("ent"), lax.axis_index("rep")
    width, rows = table_v.shape
    req, batch, rels = owner_v.shape[1], relid_v.shape[0], rel_v.shape[1]
    neg = req - 2 * batch
    slots, piece, outer = ent * CAP, rows // reps, ent // GROUP
    y, g = me // GROUP, me % GROUP
    tail, half = width - 128, width // 16 * 8 + 8
    barrier = pltpu.get_barrier_semaphore()

    def loop(start, stop, step):
        lax.fori_loop(start, stop, lambda i, c: (step(i), c)[1], 0)

    def remote(src, dst, which, p, r):
        pltpu.make_async_remote_copy(src_ref=src, dst_ref=dst, send_sem=dma.at[2 * which], recv_sem=dma.at[2 * which + 1],
                                     device_id=(p, r), device_id_type=MESH).start()

    def drain(ref, count, which, side):
        at = ref.at[pl.ds(0, count)]
        pltpu.make_async_copy(at, at, dma.at[2 * which + side]).wait()

    def greet(p, r):
        pl.semaphore_signal(barrier, inc=1, device_id=(p, r), device_id_type=MESH)

    def in_group(i):
        return y * GROUP + (g + i) % GROUP

    def in_outer(i):
        return (y + i) % outer * GROUP + g

    loop(1, GROUP, lambda i: greet(in_group(i), rep))
    loop(1, outer, lambda i: greet(in_outer(i), rep))
    loop(1, reps, lambda i: greet(me, (rep + i) % reps))
    loads = [pltpu.make_async_copy(a, b, load.at[i]) for i, (a, b) in enumerate(
        [(owner_h, owner_v), (row_h, row_v), (table_h, table_v), (filt_h, filt_v), (relid_h, relid_v), (rel_h, rel_v),
         (projt_h, projt_v), (rare_h, rare_v)])]
    for copy in loads:
        copy.start()

    loads[0].wait()
    loads[1].wait()
    owner = owner_v[...]
    named = one(iota((ent, req), 0) == owner)
    before = one(iota((req, req), 0) < iota((req, req), 1))
    rank = jnp.sum(named.astype(F32) * mm(named, before), 0, keepdims=True).astype(I32)
    slot = rank * ent + owner
    spot = owner % GROUP * (outer * CAP) + y * CAP + rank
    wide = GROUP * outer * CAP
    high, low = split(jnp.where(iota((wide, req), 0) == spot, row_v[...].reshape(1, req).astype(F32), 0.0))
    heard = one(iota((outer, req), 0) == owner // GROUP)
    ids = mm(heard, high, NT) + mm(heard, low, NT)
    for j in range(wide // 128):
        send1[:, j, :] = ids[:, j * 128 : (j + 1) * 128]
    got1[pl.ds(y, 1)] = send1[pl.ds(y, 1)]
    pl.semaphore_wait(barrier, GROUP + outer + reps - 3)
    loop(1, outer, lambda i: remote(send1.at[(y + i) % outer], got1.at[y], 0, in_outer(i), rep))
    loads[2].wait()
    loads[3].wait()
    table_high, table_low = split(table_v[...])
    band = band_matrix(filt_v[...].T)
    band_high, band_low = split(band)
    lhs_v[...] = jnp.concatenate([band_high, band_high, band_low], 1)
    bandt_v[...] = jnp.concatenate([band, band - band_high.astype(F32)], 1).T.astype(BF16)
    drain(got1, outer - 1, 0, 1)
    send2[...] = jnp.sum(got1[...], 0).reshape(wide // 128, 1, 128)
    share = GROUP * 128 // wide
    got2[pl.ds(g, 1)] = send2[pl.ds(g // share, 1)]
    loop(1, GROUP, lambda i: remote(send2.at[(g + i) % GROUP // share], got2.at[g], 1, in_group(i), rep))
    loads[4].wait()
    loads[5].wait()
    img[...] = jnp.zeros(img.shape, F32)
    strip[...] = mm(rel_v[...], one(iota((rels, batch), 0) == relid_v[...].reshape(1, batch)))
    fill_image(img, HEAD_ROWS, strip, HEAD_ROWS)
    drain(got2, GROUP - 1, 1, 1)
    src = iota((slots, GROUP), 0) % ent
    pick = one(src % GROUP == iota((slots, GROUP), 1))
    high, low = split(got2[...].reshape(GROUP, 128))
    spread = mm(pick, high) + mm(pick, low)
    at = iota((slots, 128), 0)
    keep = g % share * (outer * CAP) + at % ent // GROUP * CAP + at // ent == iota((slots, 128), 1)
    wanted = jnp.sum(jnp.where(keep, spread, 0.0), 1, keepdims=True)
    hot_rows = one(iota((slots, rows), 1).astype(F32) == wanted)
    picked = mm(hot_rows, table_high[:128], NT) + mm(hot_rows, table_low[:128], NT)
    for j in range(CAP):
        found[:, j, :] = picked[j * ent : (j + 1) * ent]
    blank = jnp.zeros((128 - tail, rows), BF16)
    picked = (mm(hot_rows, jnp.concatenate([table_high[128:], blank], 0), NT)
              + mm(hot_rows, jnp.concatenate([table_low[128:], blank], 0), NT))
    for j, piece_of in enumerate(pack_tail(picked, ent, tail)):
        found[:, CAP + j, :] = piece_of
    loop(1, ent, lambda i: remote(found.at[(me + i) % ent], fetched.at[me], 2, (me + i) % ent, rep))
    fetched[pl.ds(me, 1)] = found[pl.ds(me, 1)]

    loads[6].wait()

    def turn_over(i, c):
        at = pl.ds(pl.multiple_of(i * 512, 512), 512)
        proj_v[at, :] = projt_v[:, at].T
        return c

    lax.fori_loop(0, FILT * PER // 512, turn_over, 0)
    rel_at = pl.ds(HEAD_ROWS * PITCH, HEAD_ROWS * PITCH)
    hi_img[rel_at, :] = img[rel_at, :].astype(BF16)
    lo_img[rel_at, :] = jnp.zeros((HEAD_ROWS * PITCH, batch), BF16)

    def conv(q):
        at = pl.ds(pl.multiple_of(q * 2 * PITCH, 2 * PITCH), 4 * PITCH)
        hi, lo = hi_img[at, :], lo_img[at, :]
        v = mm(lhs_v[...], jnp.concatenate([hi, lo, hi], 0))
        s = sigmoid(v)
        a = v * s
        out = pl.ds(pl.multiple_of(q * 16, 16), 16)
        feat[:, out, :] = a.astype(BF16).reshape(FILT, 16, batch)
        dact[:, out, :] = (s + a * (1.0 - s)).reshape(FILT, 16, batch)

    loop(HEAD_PAIRS, PAIRS, conv)
    drain(fetched, ent - 1, 2, 1)

    hot = one(iota((slots, req), 0) == slot)
    high, low = split(jnp.concatenate([fetched[:, j, :] for j in range(CAP)], 0))
    val[pl.ds(0, 128), :] = mm(high, hot, TN) + mm(low, hot, TN)
    high, low = split(unpack_tail(fetched[:, CAP, :], fetched[:, CAP + 1, :], fetched[:, CAP + 2, :], tail))
    val[pl.ds(128, tail), :] = (mm(high, hot, TN) + mm(low, hot, TN))[:tail]
    strip[...] = val[:, pl.ds(0, batch)]
    fill_image(img, 0, strip, HEAD_ROWS)
    head_at = pl.ds(0, HEAD_ROWS * PITCH)
    high, low = split(img[head_at, :])
    hi_img[head_at, :] = high
    lo_img[head_at, :] = low
    for q in range(HEAD_PAIRS):
        conv(q)
    projected = mm(projt_v[...], feat[...].reshape(FILT * PER, batch))
    sig = sigmoid(projected)
    hidden = projected * sig
    pos, negs = val[:, pl.ds(batch, batch)], val[:, pl.ds(2 * batch, neg)]
    score_pos = jnp.sum(hidden * pos, 0, keepdims=True)
    score_neg = mm_hi(negs, hidden, TN)
    grad_pos = -sigmoid(-score_pos)
    grad_neg = sigmoid(score_neg) / neg
    grad_hidden = grad_pos * pos + mm_hi(negs, grad_neg)
    grad_proj = (grad_hidden * sig * (1.0 + projected * (1.0 - sig))).astype(BF16)
    val[:, pl.ds(batch, batch)] = grad_pos * hidden
    val[:, pl.ds(2 * batch, neg)] = mm_hi(hidden, grad_neg, NT)
    dimg[...] = jnp.zeros(dimg.shape, F32)

    def back(q):
        out = pl.ds(pl.multiple_of(q * 16, 16), 16)
        turned = proj_v.reshape(FILT, PER, width)[:, out, :].reshape(BAND, width)
        d = mm(turned, grad_proj) * dact[:, out, :].reshape(BAND, batch)
        return split(d)

    for q in range(HEAD_PAIRS):
        dh, dl = back(q)
        left_v[q] = jnp.concatenate([dh, dl], 1)
        both = mm(bandt_v[...], dh)
        at = pl.ds(q * 2 * PITCH, 4 * PITCH)
        dimg[at, :] += both[:64] + both[64:] + mm(bandt_v[pl.ds(0, 64), :], dl)
    for r in range(HEAD_ROWS):
        strip[pl.ds(IMG_COLS * r, IMG_COLS), :] = dimg[pl.ds(PITCH * r, IMG_COLS), :]
    val[:, pl.ds(0, batch)] = strip[...]
    high, low = split(val[...])
    packed = mm(hot, high[:128], NT) + mm(hot, low[:128], NT)
    for j in range(CAP):
        out_a[:, j, :] = packed[j * ent : (j + 1) * ent]
    loop(1, ent, lambda i: remote(out_a.at[(me + i) % ent], land_a.at[me], 3, (me + i) % ent, rep))
    blank = jnp.zeros((128 - tail, req), BF16)
    packed = (mm(hot, jnp.concatenate([high[128:], blank], 0), NT)
              + mm(hot, jnp.concatenate([low[128:], blank], 0), NT))
    for j, piece_of in enumerate(pack_tail(packed, ent, tail)):
        out_b[:, j, :] = piece_of
    loop(1, ent, lambda i: remote(out_b.at[(me + i) % ent], land_b.at[me], 11, (me + i) % ent, rep))
    land_a[pl.ds(me, 1)] = out_a[pl.ds(me, 1)]
    land_b[pl.ds(me, 1)] = out_b[pl.ds(me, 1)]

    acc_v[...] = jnp.zeros(acc_v.shape, F32)

    def add_filter(q, left):
        at = pl.ds(pl.multiple_of(q * 2 * PITCH, 2 * PITCH), 4 * PITCH)
        hi, lo = hi_img[at, :], lo_img[at, :]
        right = jnp.concatenate([jnp.concatenate([hi, hi], 1), jnp.concatenate([lo, jnp.zeros_like(lo)], 1)], 0)
        acc_v[...] += mm(left, right, NT)

    loop(0, HEAD_PAIRS, lambda q: add_filter(q, left_v[q]))
    loop(HEAD_PAIRS, PAIRS, lambda q: add_filter(q, jnp.concatenate(back(q), 1)))
    both = acc_v[...]
    acc_v[...] = both + pltpu.roll(both, 64, 1)
    taps = acc_v[pl.ds(0, FILT, stride=16), :]
    for k in range(1, 16):
        shift = k // OUT_COLS * PITCH + k % OUT_COLS
        taps = taps + pltpu.roll(acc_v[pl.ds(k, FILT, stride=16), :], 128 - shift, 1)
    turn[...] = jnp.concatenate([taps, jnp.zeros((128 - FILT, 128), F32)], 0).T
    filter_part = jnp.concatenate([turn[pl.ds(PITCH * i, 3), :] for i in range(3)] + [jnp.zeros((7, 128), F32)], 0)
    f_here[0] = filter_part
    f_x[pl.ds(rep, 1)] = filter_part[None]
    loop(1, reps, lambda i: remote(f_here.at[0], f_x.at[rep], 5, me, (rep + i) % reps))
    drain(land_a, ent - 1, 3, 1)

    def share_out(sums, here, there, which):
        for r in range(reps):
            here[r] = sums[:, r * piece : (r + 1) * piece]
        there[pl.ds(rep, 1)] = here[pl.ds(rep, 1)]
        loop(1, reps, lambda i: remote(here.at[(rep + i) % reps], there.at[rep], which, me, (rep + i) % reps))

    def columns(r):
        return pl.ds(pl.multiple_of(r * piece, piece), piece)

    high, low = split(jnp.concatenate([land_a[:, j, :] for j in range(CAP)], 0))
    share_out(mm(high, hot_rows, TN) + mm(low, hot_rows, TN), part_a, pland_a, 4)
    drain(land_b, ent - 1, 11, 1)
    high, low = split(unpack_tail(land_b[:, 0, :], land_b[:, 1, :], land_b[:, 2, :], tail))
    share_out((mm(high, hot_rows, TN) + mm(low, hot_rows, TN))[:tail], part_b, pland_b, 12)
    drain(f_x, reps - 1, 5, 1)
    f_here[1] = jnp.sum(f_x[...], 0)
    f_g[pl.ds(g, 1)] = f_here[pl.ds(1, 1)]
    loop(1, GROUP, lambda i: remote(f_here.at[1], f_g.at[g], 6, in_group(i), rep))
    drain(pland_a, reps - 1, 4, 1)
    drain(pland_b, reps - 1, 12, 1)
    block = table_v[:, columns(rep)] - learn_rate * jnp.concatenate([jnp.sum(pland_a[...], 0), jnp.sum(pland_b[...], 0)], 0)
    n_here[0] = jnp.sqrt(jnp.sum(block * block, 0, keepdims=True) + norm_eps)
    upd[:, columns(rep)] = block
    n_a[pl.ds(rep * outer + y, 1)] = n_here[pl.ds(0, 1)]
    loop(1, reps * outer, lambda i: remote(n_here.at[0], n_a.at[rep * outer + y], 9, in_outer(i), (rep + i // outer) % reps))
    right, left = (rep + 1) % reps, (rep + reps - 1) % reps
    upper, lower = pl.ds(0, half), pl.ds(half, width - half)

    def pass_on(at, r, which, to):
        remote(upd.at[at, columns(r)], upd.at[at, columns(r)], which, me, to)

    def arrived(at, r, which, side):
        ref = upd.at[at, columns(r)]
        pltpu.make_async_copy(ref, ref, dma.at[2 * which + side]).wait()

    everything = pl.ds(0, width)
    pass_on(everything, rep, 8, right)
    pass_on(everything, rep, 13, left)
    drain(f_g, GROUP - 1, 6, 1)
    f_here[2] = jnp.sum(f_g[...], 0)
    f_y[pl.ds(y, 1)] = f_here[pl.ds(2, 1)]
    loop(1, outer, lambda i: remote(f_here.at[2], f_y.at[y], 7, in_outer(i), rep))
    arrived(everything, left, 8, 1)
    pass_on(upper, left, 14, right)
    arrived(everything, right, 13, 1)
    pass_on(lower, right, 15, left)
    drain(n_a, reps * outer - 1, 9, 1)
    n_here[1] = jnp.sum(n_a[...], 0)
    n_b[pl.ds(g, 1)] = n_here[pl.ds(1, 1)]
    loop(1, GROUP, lambda i: remote(n_here.at[1], n_b.at[g], 10, in_group(i), rep))
    far = (rep + 2) % reps
    arrived(upper, far, 14, 1)
    arrived(lower, far, 15, 1)
    updated = upd[...]
    norm = jnp.sqrt(jnp.sum(updated * updated, 0, keepdims=True) + norm_eps)
    loads[7].wait()
    drain(f_y, outer - 1, 7, 1)
    total_ref[...] = jnp.sum(f_y[...], 0)
    drain(send1, outer - 1, 0, 0)
    drain(got2, GROUP - 1, 1, 0)
    drain(found, ent - 1, 2, 0)
    drain(out_a, ent - 1, 3, 0)
    drain(out_b, ent - 1, 11, 0)
    drain(part_a, reps - 1, 4, 0)
    drain(part_b, reps - 1, 12, 0)
    drain(f_x, reps - 1, 5, 0)
    drain(f_g, GROUP - 1, 6, 0)
    drain(f_y, outer - 1, 7, 0)
    arrived(everything, rep, 8, 0)
    arrived(everything, rep, 13, 0)
    arrived(upper, left, 14, 0)
    arrived(lower, right, 15, 0)
    drain(n_a, reps * outer - 1, 9, 0)
    drain(n_b, GROUP - 1, 10, 1)
    drain(n_b, GROUP - 1, 10, 0)
    norm_total = jnp.sum(jnp.sum(n_b[...], 0), 1, keepdims=True)
    target = 0.25 * run_ref[...] + 0.75 * norm_total / (rows * ent)
    out_ref[...] = updated * jnp.where(rare_v[...].reshape(1, rows) == 1, target / norm, 1.0)


def step(owner, row, relid, rare, run, table_t, rel_t, filt, proj_t, ent, reps):
    width, rows = table_t.shape
    req, batch, feats = owner.shape[1], relid.shape[0], proj_t.shape[1]
    piece, outer = rows // reps, ent // GROUP
    vmem, hbm = pl.BlockSpec(memory_space=pltpu.VMEM), pl.BlockSpec(memory_space=pltpu.HBM)
    v = pltpu.VMEM
    wide = GROUP * outer * CAP
    exchange, first, second = v((ent, CAP + 3, 128), F32), v((ent, CAP, 128), F32), v((ent, 3, 128), F32)
    return pl.pallas_call(
        functools.partial(step_kernel, ent, reps),
        out_shape=(jax.ShapeDtypeStruct((width, rows), F32), jax.ShapeDtypeStruct((16, 128), F32)),
        in_specs=[hbm] * 4 + [vmem] + [hbm] * 4, out_specs=(vmem,) * 2,
        scratch_shapes=[
            v(owner.shape, I32), v(row.shape, I32), v(relid.shape, I32), v(rare.shape, I32), v((width, rows), F32),
            v(rel_t.shape, BF16), v(filt.shape, F32), v(proj_t.shape, BF16),
            v((feats, width), BF16), v((outer, wide // 128, 128), F32), v((outer, wide // 128, 128), F32),
            v((wide // 128, 1, 128), F32), v((GROUP, 1, 128), F32), exchange, exchange, first, second, first, second,
            v((width, req), F32), v((width, batch), F32), v((IMG_ROWS * PITCH, batch), F32),
            v((IMG_ROWS * PITCH, batch), BF16), v((IMG_ROWS * PITCH, batch), BF16), v((BAND, 192), BF16),
            v((128, BAND), BF16), v((FILT, PER, batch), BF16), v((FILT, PER, batch), F32),
            v((HEAD_PAIRS, BAND, 2 * batch), BF16), v(((HEAD_ROWS + 2) * PITCH, batch), F32), v((BAND, 128), F32),
            v((128, 128), F32),
            v((reps, 128, piece), F32), v((reps, width - 128, piece), F32),
            v((reps, 128, piece), F32), v((reps, width - 128, piece), F32), v((width, rows), F32), v((3, 16, 128), F32),
            v((reps, 16, 128), F32), v((GROUP, 16, 128), F32), v((outer, 16, 128), F32),
            v((2, 1, 128), F32), v((reps * outer, 1, 128), F32), v((GROUP, 1, 128), F32),
            pltpu.SemaphoreType.DMA((8,)), pltpu.SemaphoreType.DMA((32,))],
        compiler_params=pltpu.CompilerParams(collective_id=0, has_side_effects=True, vmem_limit_bytes=44 << 20),
        name="step",
    )(*[pltpu.with_memory_space_constraint(a, pltpu.HBM) for a in (owner, row, relid, rare)], run, *[pltpu.with_memory_space_constraint(a, pltpu.HBM) for a in (table_t, rel_t, filt, proj_t)])


def body(entity_table, relation_table, filters, projection, request_owner, request_row, relation_id, rare_flag, running_norm):
    ent, reps = lax.axis_size("ent"), lax.axis_size("rep")
    batch, req = relation_id.shape[0], request_row.shape[0]
    new_t, total = step(request_owner.reshape(1, req), request_row, relation_id, rare_flag, running_norm.reshape(1, 1),
                        entity_table.T, relation_table.T, filters.T, projection.T, ent, reps)
    filter_grad = total[:9, :FILT].T / (batch * ent * reps)
    return new_t.T, filter_grad


def solution(mesh):
    in_specs = (P("ent", None), P(), P(), P(), P(("ent", "rep"), None), P(("ent", "rep")), P(("ent", "rep")), P("ent"), P())
    return jax.shard_map(body, mesh=mesh, in_specs=in_specs, out_specs=(P("ent", None), P()), check_vma=False)
```

```python
import functools
import jax
import jax.numpy as jnp
from jax import lax
from jax.experimental import pallas as pl
from jax.experimental.pallas import tpu as pltpu
from jax.sharding import PartitionSpec as P

MESH = pl.DeviceIdType.MESH
HI = lax.Precision.HIGHEST
F32, BF16, I32 = jnp.float32, jnp.bfloat16, jnp.int32
NN = (((1,), (0,)), ((), ()))
NT = (((1,), (1,)), ((), ()))
TN = (((0,), (0,)), ((), ()))
learn_rate, norm_eps = 0.5, 1e-06
FILT, OUT_ROWS, OUT_COLS, IMG_ROWS, IMG_COLS, PITCH = 32, 38, 8, 40, 10, 16
HEAD_ROWS = 20
PAIRS, HEAD_PAIRS = OUT_ROWS // 2, HEAD_ROWS // 2
PER = OUT_ROWS * OUT_COLS
BAND = FILT * 16
CAP, GROUP = 4, 16


def iota(shape, dim):
    return lax.broadcasted_iota(I32, shape, dim)


def mm(a, b, dims=NN):
    return lax.dot_general(a, b, dims, preferred_element_type=F32)


def mm_hi(a, b, dims=NN):
    return lax.dot_general(a, b, dims, precision=HI, preferred_element_type=F32)


def split(v):
    high = v.astype(BF16)
    return high, (v - high.astype(F32)).astype(BF16)


def one(mask):
    return mask.astype(F32).astype(BF16)


def sigmoid(v):
    return 0.5 * jnp.tanh(0.5 * v) + 0.5


def band_matrix(filt):
    r, k = iota((16, 64), 0), iota((16, 64), 1)
    di, dj = k // PITCH - r // OUT_COLS, k % PITCH - r % OUT_COLS
    total = jnp.zeros((FILT, 16, 64), F32)
    for t in range(9):
        mask = ((di == t // 3) & (dj == t % 3)).astype(F32)
        total = total + filt[:, t : t + 1][:, :, None] * mask[None]
    return total.reshape(BAND, 64)


def pack_tail(t, ent, tail):
    lane = iota((ent, 128), 1)
    t0, t1, t2, t3 = [t[i * ent : (i + 1) * ent] for i in range(CAP)]
    return (jnp.where(lane < tail, t0, pltpu.roll(t3, tail, 1)),
            jnp.where(lane < tail, t1, pltpu.roll(t3, 2 * tail - 128, 1)), t2)


def unpack_tail(r0, r1, r2, tail):
    lane = iota(r0.shape, 1)
    t3 = jnp.where(lane < 128 - tail, pltpu.roll(r0, 128 - tail, 1), pltpu.roll(r1, 256 - 2 * tail, 1))
    return jnp.concatenate([r0, r1, r2, t3], 0)


def fill_image(img, base, strip, rows):
    for r in range(rows):
        img[pl.ds(PITCH * (base + r), IMG_COLS), :] = strip[pl.ds(IMG_COLS * r, IMG_COLS), :]


def step_kernel(ent, reps, *refs):
    (owner_h, row_h, relid_h, rare_h, run_ref, table_h, rel_h, filt_h, projt_h, out_ref, total_ref,
     owner_v, row_v, relid_v, rare_v, table_v, rel_v, filt_v, projt_v,
     proj_v, send1, got1, send2, got2, found, fetched, out_a, out_b, land_a, land_b,
     val, strip, img, hi_img, lo_img, lhs_v, bandt_v, feat, dact, left_v, dimg, acc_v, turn,
     part_a, part_b, pland_a, pland_b, upd, f_here, f_x, f_g, f_y, n_here, n_a, n_b, load, dma) = refs
    me, rep = lax.axis_index("ent"), lax.axis_index("rep")
    width, rows = table_v.shape
    req, batch, rels = owner_v.shape[1], relid_v.shape[0], rel_v.shape[1]
    neg = req - 2 * batch
    slots, piece, outer = ent * CAP, rows // reps, ent // GROUP
    y, g = me // GROUP, me % GROUP
    tail, half = width - 128, width // 16 * 8 + 8
    barrier = pltpu.get_barrier_semaphore()

    def loop(start, stop, step):
        lax.fori_loop(start, stop, lambda i, c: (step(i), c)[1], 0)

    def remote(src, dst, which, p, r):
        pltpu.make_async_remote_copy(src_ref=src, dst_ref=dst, send_sem=dma.at[2 * which], recv_sem=dma.at[2 * which + 1],
                                     device_id=(p, r), device_id_type=MESH).start()

    def drain(ref, count, which, side):
        at = ref.at[pl.ds(0, count)]
        pltpu.make_async_copy(at, at, dma.at[2 * which + side]).wait()

    def greet(p, r):
        pl.semaphore_signal(barrier, inc=1, device_id=(p, r), device_id_type=MESH)

    def in_group(i):
        return y * GROUP + (g + i) % GROUP

    def in_outer(i):
        return (y + i) % outer * GROUP + g

    loop(1, GROUP, lambda i: greet(in_group(i), rep))
    loop(1, outer, lambda i: greet(in_outer(i), rep))
    loop(1, reps, lambda i: greet(me, (rep + i) % reps))
    loads = [pltpu.make_async_copy(a, b, load.at[i]) for i, (a, b) in enumerate(
        [(owner_h, owner_v), (row_h, row_v), (table_h, table_v), (filt_h, filt_v), (relid_h, relid_v), (rel_h, rel_v),
         (projt_h, projt_v), (rare_h, rare_v)])]
    for copy in loads:
        copy.start()

    loads[0].wait()
    loads[1].wait()
    owner = owner_v[...]
    named = one(iota((ent, req), 0) == owner)
    before = one(iota((req, req), 0) < iota((req, req), 1))
    rank = jnp.sum(named.astype(F32) * mm(named, before), 0, keepdims=True).astype(I32)
    slot = rank * ent + owner
    spot = owner % GROUP * (outer * CAP) + y * CAP + rank
    wide = GROUP * outer * CAP
    high, low = split(jnp.where(iota((wide, req), 0) == spot, row_v[...].reshape(1, req).astype(F32), 0.0))
    heard = one(iota((outer, req), 0) == owner // GROUP)
    ids = mm(heard, high, NT) + mm(heard, low, NT)
    for j in range(wide // 128):
        send1[:, j, :] = ids[:, j * 128 : (j + 1) * 128]
    got1[pl.ds(y, 1)] = send1[pl.ds(y, 1)]
    pl.semaphore_wait(barrier, GROUP + outer + reps - 3)
    loop(1, outer, lambda i: remote(send1.at[(y + i) % outer], got1.at[y], 0, in_outer(i), rep))
    loads[2].wait()
    table_high, table_low = split(table_v[...])
    drain(got1, outer - 1, 0, 1)
    send2[...] = jnp.sum(got1[...], 0).reshape(wide // 128, 1, 128)
    share = GROUP * 128 // wide
    got2[pl.ds(g, 1)] = send2[pl.ds(g // share, 1)]
    loop(1, GROUP, lambda i: remote(send2.at[(g + i) % GROUP // share], got2.at[g], 1, in_group(i), rep))
    drain(got2, GROUP - 1, 1, 1)
    src = iota((slots, GROUP), 0) % ent
    pick = one(src % GROUP == iota((slots, GROUP), 1))
    high, low = split(got2[...].reshape(GROUP, 128))
    spread = mm(pick, high) + mm(pick, low)
    at = iota((slots, 128), 0)
    keep = g % share * (outer * CAP) + at % ent // GROUP * CAP + at // ent == iota((slots, 128), 1)
    wanted = jnp.sum(jnp.where(keep, spread, 0.0), 1, keepdims=True)
    hot_rows = one(iota((slots, rows), 1).astype(F32) == wanted)
    picked = mm(hot_rows, table_high[:128], NT) + mm(hot_rows, table_low[:128], NT)
    for j in range(CAP):
        found[:, j, :] = picked[j * ent : (j + 1) * ent]
    blank = jnp.zeros((128 - tail, rows), BF16)
    picked = (mm(hot_rows, jnp.concatenate([table_high[128:], blank], 0), NT)
              + mm(hot_rows, jnp.concatenate([table_low[128:], blank], 0), NT))
    for j, piece_of in enumerate(pack_tail(picked, ent, tail)):
        found[:, CAP + j, :] = piece_of
    loop(1, ent, lambda i: remote(found.at[(me + i) % ent], fetched.at[me], 2, (me + i) % ent, rep))
    fetched[pl.ds(me, 1)] = found[pl.ds(me, 1)]

    loads[3].wait()
    band = band_matrix(filt_v[...].T)
    band_high, band_low = split(band)
    lhs_v[...] = jnp.concatenate([band_high, band_high, band_low], 1)
    bandt_v[...] = jnp.concatenate([band, band - band_high.astype(F32)], 1).T.astype(BF16)
    loads[4].wait()
    loads[5].wait()
    img[...] = jnp.zeros(img.shape, F32)
    strip[...] = mm(rel_v[...], one(iota((rels, batch), 0) == relid_v[...].reshape(1, batch)))
    fill_image(img, HEAD_ROWS, strip, HEAD_ROWS)
    loads[6].wait()

    def turn_over(i, c):
        at = pl.ds(pl.multiple_of(i * 512, 512), 512)
        proj_v[at, :] = projt_v[:, at].T
        return c

    lax.fori_loop(0, FILT * PER // 512, turn_over, 0)
    rel_at = pl.ds(HEAD_ROWS * PITCH, HEAD_ROWS * PITCH)
    hi_img[rel_at, :] = img[rel_at, :].astype(BF16)
    lo_img[rel_at, :] = jnp.zeros((HEAD_ROWS * PITCH, batch), BF16)

    def conv(q):
        at = pl.ds(pl.multiple_of(q * 2 * PITCH, 2 * PITCH), 4 * PITCH)
        hi, lo = hi_img[at, :], lo_img[at, :]
        v = mm(lhs_v[...], jnp.concatenate([hi, lo, hi], 0))
        s = sigmoid(v)
        a = v * s
        out = pl.ds(pl.multiple_of(q * 16, 16), 16)
        feat[:, out, :] = a.astype(BF16).reshape(FILT, 16, batch)
        dact[:, out, :] = (s + a * (1.0 - s)).reshape(FILT, 16, batch)

    def conv_two(q):
        def stack(k):
            at = pl.ds(k * 2 * PITCH, 4 * PITCH)
            hi, lo = hi_img[at, :], lo_img[at, :]
            return jnp.concatenate([hi, lo, hi], 0)

        v = mm(lhs_v[...], jnp.concatenate([stack(q), stack(q + 1)], 1))
        s = sigmoid(v)
        a = v * s
        d = s + a * (1.0 - s)
        for k in range(2):
            out, lanes = pl.ds((q + k) * 16, 16), slice(k * batch, (k + 1) * batch)
            feat[:, out, :] = a[:, lanes].astype(BF16).reshape(FILT, 16, batch)
            dact[:, out, :] = d[:, lanes].reshape(FILT, 16, batch)

    loop(HEAD_PAIRS, PAIRS, conv)
    drain(fetched, ent - 1, 2, 1)

    hot = one(iota((slots, req), 0) == slot)
    high, low = split(jnp.concatenate([fetched[:, j, :] for j in range(CAP)], 0))
    val[pl.ds(0, 128), :] = mm(high, hot, TN) + mm(low, hot, TN)
    high, low = split(unpack_tail(fetched[:, CAP, :], fetched[:, CAP + 1, :], fetched[:, CAP + 2, :], tail))
    val[pl.ds(128, tail), :] = (mm(high, hot, TN) + mm(low, hot, TN))[:tail]
    strip[...] = val[:, pl.ds(0, batch)]
    fill_image(img, 0, strip, HEAD_ROWS)
    head_at = pl.ds(0, HEAD_ROWS * PITCH)
    high, low = split(img[head_at, :])
    hi_img[head_at, :] = high
    lo_img[head_at, :] = low
    for q in range(0, HEAD_PAIRS, 2):
        conv_two(q)
    projected = mm(projt_v[...], feat[...].reshape(FILT * PER, batch))
    sig = sigmoid(projected)
    hidden = projected * sig
    pos, negs = val[:, pl.ds(batch, batch)], val[:, pl.ds(2 * batch, neg)]
    score_pos = jnp.sum(hidden * pos, 0, keepdims=True)
    score_neg = mm_hi(negs, hidden, TN)
    grad_pos = -sigmoid(-score_pos)
    grad_neg = sigmoid(score_neg) / neg
    grad_hidden = grad_pos * pos + mm_hi(negs, grad_neg)
    grad_proj = (grad_hidden * sig * (1.0 + projected * (1.0 - sig))).astype(BF16)
    val[:, pl.ds(batch, batch)] = grad_pos * hidden
    val[:, pl.ds(2 * batch, neg)] = mm_hi(hidden, grad_neg, NT)
    dimg[...] = jnp.zeros(dimg.shape, F32)

    def back(q):
        out = pl.ds(pl.multiple_of(q * 16, 16), 16)
        turned = proj_v.reshape(FILT, PER, width)[:, out, :].reshape(BAND, width)
        d = mm(turned, grad_proj) * dact[:, out, :].reshape(BAND, batch)
        return split(d)

    def head_back(first, last):
        for q in range(first, last):
            left = jnp.concatenate(back(q), 1)
            left_v[q] = left
            both = mm(bandt_v[...], left)
            at = pl.ds(q * 2 * PITCH, 4 * PITCH)
            dimg[at, :] += both[:64, :batch] + both[64:, :batch] + both[:64, batch:]

    def head_rows(first, last):
        for r in range(first, last):
            strip[pl.ds(IMG_COLS * r, IMG_COLS), :] = dimg[pl.ds(PITCH * r, IMG_COLS), :]

    cut_pair = (128 // IMG_COLS + 2) // 2
    cut_row = 128 // IMG_COLS + 1
    head_back(0, cut_pair)
    head_rows(0, cut_row)
    val[pl.ds(0, 128), pl.ds(0, batch)] = strip[pl.ds(0, 128), :]
    high, low = split(val[pl.ds(0, 128), :])
    packed = mm(hot, high, NT) + mm(hot, low, NT)
    for j in range(CAP):
        out_a[:, j, :] = packed[j * ent : (j + 1) * ent]
    loop(1, ent, lambda i: remote(out_a.at[(me + i) % ent], land_a.at[me], 3, (me + i) % ent, rep))
    head_back(cut_pair, HEAD_PAIRS)
    head_rows(cut_row, HEAD_ROWS)
    val[pl.ds(128, tail), pl.ds(0, batch)] = strip[pl.ds(128, tail), :]
    high, low = split(val[pl.ds(128, tail), :])
    blank = jnp.zeros((128 - tail, req), BF16)
    packed = (mm(hot, jnp.concatenate([high, blank], 0), NT) + mm(hot, jnp.concatenate([low, blank], 0), NT))
    for j, piece_of in enumerate(pack_tail(packed, ent, tail)):
        out_b[:, j, :] = piece_of
    loop(1, ent, lambda i: remote(out_b.at[(me + i) % ent], land_b.at[me], 11, (me + i) % ent, rep))
    land_a[pl.ds(me, 1)] = out_a[pl.ds(me, 1)]
    land_b[pl.ds(me, 1)] = out_b[pl.ds(me, 1)]

    acc_v[...] = jnp.zeros(acc_v.shape, F32)

    def add_filter(q, left):
        at = pl.ds(pl.multiple_of(q * 2 * PITCH, 2 * PITCH), 4 * PITCH)
        hi, lo = hi_img[at, :], lo_img[at, :]
        right = jnp.concatenate([jnp.concatenate([hi, hi], 1), jnp.concatenate([lo, jnp.zeros_like(lo)], 1)], 0)
        acc_v[...] += mm(left, right, NT)

    loop(0, HEAD_PAIRS, lambda q: add_filter(q, left_v[q]))
    loop(HEAD_PAIRS, PAIRS, lambda q: add_filter(q, jnp.concatenate(back(q), 1)))
    both = acc_v[...]
    acc_v[...] = both + pltpu.roll(both, 64, 1)
    taps = acc_v[pl.ds(0, FILT, stride=16), :]
    for k in range(1, 16):
        shift = k // OUT_COLS * PITCH + k % OUT_COLS
        taps = taps + pltpu.roll(acc_v[pl.ds(k, FILT, stride=16), :], 128 - shift, 1)
    turn[...] = jnp.concatenate([taps, jnp.zeros((128 - FILT, 128), F32)], 0).T
    filter_part = jnp.concatenate(
        [sum(pltpu.roll(turn[pl.ds(PITCH * i + j, 1), :], FILT * j, 1) for j in range(3)) for i in range(3)], 0)
    f_here[0] = filter_part
    f_x[pl.ds(rep, 1)] = filter_part[None]
    loop(1, reps, lambda i: remote(f_here.at[0], f_x.at[rep], 5, me, (rep + i) % reps))
    drain(land_a, ent - 1, 3, 1)

    def share_out(sums, here, there, which):
        for r in range(reps):
            here[r] = sums[:, r * piece : (r + 1) * piece]
        there[pl.ds(rep, 1)] = here[pl.ds(rep, 1)]
        loop(1, reps, lambda i: remote(here.at[(rep + i) % reps], there.at[rep], which, me, (rep + i) % reps))

    def columns(r):
        return pl.ds(pl.multiple_of(r * piece, piece), piece)

    high, low = split(jnp.concatenate([land_a[:, j, :] for j in range(CAP)], 0))
    share_out(mm(high, hot_rows, TN) + mm(low, hot_rows, TN), part_a, pland_a, 4)
    drain(land_b, ent - 1, 11, 1)
    high, low = split(unpack_tail(land_b[:, 0, :], land_b[:, 1, :], land_b[:, 2, :], tail))
    share_out((mm(high, hot_rows, TN) + mm(low, hot_rows, TN))[:tail], part_b, pland_b, 12)
    drain(f_x, reps - 1, 5, 1)
    f_here[1] = jnp.sum(f_x[...], 0)
    f_g[pl.ds(g, 1)] = f_here[pl.ds(1, 1)]
    loop(1, GROUP, lambda i: remote(f_here.at[1], f_g.at[g], 6, in_group(i), rep))
    drain(pland_a, reps - 1, 4, 1)
    drain(pland_b, reps - 1, 12, 1)
    block = table_v[:, columns(rep)] - learn_rate * jnp.concatenate([jnp.sum(pland_a[...], 0), jnp.sum(pland_b[...], 0)], 0)
    n_here[0] = jnp.sqrt(jnp.sum(block * block, 0, keepdims=True) + norm_eps)
    upd[:, columns(rep)] = block
    n_a[pl.ds(rep * outer + y, 1)] = n_here[pl.ds(0, 1)]
    loop(1, reps * outer, lambda i: remote(n_here.at[0], n_a.at[rep * outer + y], 9, in_outer(i), (rep + i // outer) % reps))
    right, left = (rep + 1) % reps, (rep + reps - 1) % reps
    upper, lower = pl.ds(0, half), pl.ds(half, width - half)

    def pass_on(at, r, which, to):
        remote(upd.at[at, columns(r)], upd.at[at, columns(r)], which, me, to)

    def arrived(at, r, which, side):
        ref = upd.at[at, columns(r)]
        pltpu.make_async_copy(ref, ref, dma.at[2 * which + side]).wait()

    everything = pl.ds(0, width)
    pass_on(everything, rep, 8, right)
    pass_on(everything, rep, 13, left)
    drain(f_g, GROUP - 1, 6, 1)
    f_here[2] = jnp.sum(f_g[...], 0)
    f_y[pl.ds(y, 1)] = f_here[pl.ds(2, 1)]
    loop(1, outer, lambda i: remote(f_here.at[2], f_y.at[y], 7, in_outer(i), rep))
    arrived(everything, left, 8, 1)
    pass_on(upper, left, 14, right)
    arrived(everything, right, 13, 1)
    pass_on(lower, right, 15, left)
    drain(n_a, reps * outer - 1, 9, 1)
    n_here[1] = jnp.sum(n_a[...], 0)
    n_b[pl.ds(g, 1)] = n_here[pl.ds(1, 1)]
    loop(1, GROUP, lambda i: remote(n_here.at[1], n_b.at[g], 10, in_group(i), rep))
    far = (rep + 2) % reps
    arrived(upper, far, 14, 1)
    arrived(lower, far, 15, 1)
    updated = upd[...]
    norm = jnp.sqrt(jnp.sum(updated * updated, 0, keepdims=True) + norm_eps)
    loads[7].wait()
    drain(f_y, outer - 1, 7, 1)
    total_ref[...] = jnp.sum(f_y[...], 0)
    drain(send1, outer - 1, 0, 0)
    drain(got2, GROUP - 1, 1, 0)
    drain(found, ent - 1, 2, 0)
    drain(out_a, ent - 1, 3, 0)
    drain(out_b, ent - 1, 11, 0)
    drain(part_a, reps - 1, 4, 0)
    drain(part_b, reps - 1, 12, 0)
    drain(f_x, reps - 1, 5, 0)
    drain(f_g, GROUP - 1, 6, 0)
    drain(f_y, outer - 1, 7, 0)
    arrived(everything, rep, 8, 0)
    arrived(everything, rep, 13, 0)
    arrived(upper, left, 14, 0)
    arrived(lower, right, 15, 0)
    drain(n_a, reps * outer - 1, 9, 0)
    drain(n_b, GROUP - 1, 10, 1)
    drain(n_b, GROUP - 1, 10, 0)
    norm_total = jnp.sum(jnp.sum(n_b[...], 0), 1, keepdims=True)
    target = 0.25 * run_ref[...] + 0.75 * norm_total / (rows * ent)
    out_ref[...] = updated * jnp.where(rare_v[...].reshape(1, rows) == 1, target / norm, 1.0)


def step(owner, row, relid, rare, run, table_t, rel_t, filt, proj_t, ent, reps):
    width, rows = table_t.shape
    req, batch, feats = owner.shape[1], relid.shape[0], proj_t.shape[1]
    piece, outer = rows // reps, ent // GROUP
    vmem, hbm = pl.BlockSpec(memory_space=pltpu.VMEM), pl.BlockSpec(memory_space=pltpu.HBM)
    v = pltpu.VMEM
    wide = GROUP * outer * CAP
    exchange, first, second = v((ent, CAP + 3, 128), F32), v((ent, CAP, 128), F32), v((ent, 3, 128), F32)
    return pl.pallas_call(
        functools.partial(step_kernel, ent, reps),
        out_shape=(jax.ShapeDtypeStruct((width, rows), F32), jax.ShapeDtypeStruct((3, 128), F32)),
        in_specs=[hbm] * 4 + [vmem] + [hbm] * 4, out_specs=(vmem,) * 2,
        scratch_shapes=[
            v(owner.shape, I32), v(row.shape, I32), v(relid.shape, I32), v(rare.shape, I32), v((width, rows), F32),
            v(rel_t.shape, BF16), v(filt.shape, F32), v(proj_t.shape, BF16),
            v((feats, width), BF16), v((outer, wide // 128, 128), F32), v((outer, wide // 128, 128), F32),
            v((wide // 128, 1, 128), F32), v((GROUP, 1, 128), F32), exchange, exchange, first, second, first, second,
            v((width, req), F32), v((width, batch), F32), v((IMG_ROWS * PITCH, batch), F32),
            v((IMG_ROWS * PITCH, batch), BF16), v((IMG_ROWS * PITCH, batch), BF16), v((BAND, 192), BF16),
            v((128, BAND), BF16), v((FILT, PER, batch), BF16), v((FILT, PER, batch), F32),
            v((HEAD_PAIRS, BAND, 2 * batch), BF16), v(((HEAD_ROWS + 2) * PITCH, batch), F32), v((BAND, 128), F32),
            v((128, 128), F32),
            v((reps, 128, piece), F32), v((reps, width - 128, piece), F32),
            v((reps, 128, piece), F32), v((reps, width - 128, piece), F32), v((width, rows), F32), v((3, 3, 128), F32),
            v((reps, 3, 128), F32), v((GROUP, 3, 128), F32), v((outer, 3, 128), F32),
            v((2, 1, 128), F32), v((reps * outer, 1, 128), F32), v((GROUP, 1, 128), F32),
            pltpu.SemaphoreType.DMA((8,)), pltpu.SemaphoreType.DMA((32,))],
        compiler_params=pltpu.CompilerParams(collective_id=0, has_side_effects=True, vmem_limit_bytes=44 << 20),
        name="step",
    )(*[pltpu.with_memory_space_constraint(a, pltpu.HBM) for a in (owner, row, relid, rare)], run, *[pltpu.with_memory_space_constraint(a, pltpu.HBM) for a in (table_t, rel_t, filt, proj_t)])


def body(entity_table, relation_table, filters, projection, request_owner, request_row, relation_id, rare_flag, running_norm):
    ent, reps = lax.axis_size("ent"), lax.axis_size("rep")
    batch, req = relation_id.shape[0], request_row.shape[0]
    new_t, total = step(request_owner.reshape(1, req), request_row, relation_id, rare_flag, running_norm.reshape(1, 1),
                        entity_table.T, relation_table.T, filters.T, projection.T, ent, reps)
    filter_grad = total[:, : 3 * FILT].reshape(9, FILT).T / (batch * ent * reps)
    return new_t.T, filter_grad


def solution(mesh):
    in_specs = (P("ent", None), P(), P(), P(), P(("ent", "rep"), None), P(("ent", "rep")), P(("ent", "rep")), P("ent"), P())
    return jax.shard_map(body, mesh=mesh, in_specs=in_specs, out_specs=(P("ent", None), P()), check_vma=False)
```

```python
import functools
import jax
import jax.numpy as jnp
from jax import lax
from jax.experimental import pallas as pl
from jax.experimental.pallas import tpu as pltpu
from jax.sharding import PartitionSpec as P

MESH = pl.DeviceIdType.MESH
HI = lax.Precision.HIGHEST
F32, BF16, I32 = jnp.float32, jnp.bfloat16, jnp.int32
NN = (((1,), (0,)), ((), ()))
NT = (((1,), (1,)), ((), ()))
TN = (((0,), (0,)), ((), ()))
learn_rate, norm_eps = 0.5, 1e-06
FILT, OUT_ROWS, OUT_COLS, IMG_ROWS, IMG_COLS, PITCH = 32, 38, 8, 40, 10, 16
HEAD_ROWS = 20
PAIRS, HEAD_PAIRS = OUT_ROWS // 2, HEAD_ROWS // 2
PER = OUT_ROWS * OUT_COLS
BAND = FILT * 16
CAP, GROUP = 4, 16


def iota(shape, dim):
    return lax.broadcasted_iota(I32, shape, dim)


def mm(a, b, dims=NN):
    return lax.dot_general(a, b, dims, preferred_element_type=F32)


def mm_hi(a, b, dims=NN):
    (ah, al), (bh, bl) = split(a), split(b)
    return mm(ah, bh, dims) + (mm(ah, bl, dims) + mm(al, bh, dims))


def split(v):
    high = v.astype(BF16)
    return high, (v - high.astype(F32)).astype(BF16)


def one(mask):
    return mask.astype(F32).astype(BF16)


def sigmoid(v):
    return 0.5 * jnp.tanh(0.5 * v) + 0.5


def band_matrix(filt):
    r, k = iota((16, 64), 0), iota((16, 64), 1)
    di, dj = k // PITCH - r // OUT_COLS, k % PITCH - r % OUT_COLS
    total = jnp.zeros((FILT, 16, 64), F32)
    for t in range(9):
        mask = ((di == t // 3) & (dj == t % 3)).astype(F32)
        total = total + filt[:, t : t + 1][:, :, None] * mask[None]
    return total.reshape(BAND, 64)


def pack_tail(t, ent, tail):
    lane = iota((ent, 128), 1)
    t0, t1, t2, t3 = [t[i * ent : (i + 1) * ent] for i in range(CAP)]
    return (jnp.where(lane < tail, t0, pltpu.roll(t3, tail, 1)),
            jnp.where(lane < tail, t1, pltpu.roll(t3, 2 * tail - 128, 1)), t2)


def unpack_tail(r0, r1, r2, tail):
    lane = iota(r0.shape, 1)
    t3 = jnp.where(lane < 128 - tail, pltpu.roll(r0, 128 - tail, 1), pltpu.roll(r1, 256 - 2 * tail, 1))
    return jnp.concatenate([r0, r1, r2, t3], 0)


def fill_image(img, base, strip, rows):
    for r in range(rows):
        img[pl.ds(PITCH * (base + r), IMG_COLS), :] = strip[pl.ds(IMG_COLS * r, IMG_COLS), :]


def step_kernel(ent, reps, *refs):
    (owner_h, row_h, relid_h, rare_h, run_ref, table_h, rel_h, filt_h, projt_h, out_ref, total_ref,
     owner_v, row_v, relid_v, rare_v, table_v, rel_v, filt_v, projt_v,
     proj_v, send1, got1, send2, got2, found, found_b, fetched, fetched_b, out_a, out_b, land_a, land_b,
     val, strip, img, hi_img, lo_img, lhs_v, bandt_v, feat, dact, left_v, dimg, acc_v, turn,
     part_a, part_b, pland_a, pland_b, upd, f_here, f_x, f_g, f_y, n_here, n_a, n_b, load, dma) = refs
    me, rep = lax.axis_index("ent"), lax.axis_index("rep")
    width, rows = table_v.shape
    req, batch, rels = owner_v.shape[1], relid_v.shape[0], rel_v.shape[1]
    neg = req - 2 * batch
    slots, piece, outer = ent * CAP, rows // reps, ent // GROUP
    y, g = me // GROUP, me % GROUP
    tail, half = width - 128, width // 16 * 8 + 8
    barrier = pltpu.get_barrier_semaphore()

    def loop(start, stop, step):
        lax.fori_loop(start, stop, lambda i, c: (step(i), c)[1], 0)

    def remote(src, dst, which, p, r):
        pltpu.make_async_remote_copy(src_ref=src, dst_ref=dst, send_sem=dma.at[2 * which], recv_sem=dma.at[2 * which + 1],
                                     device_id=(p, r), device_id_type=MESH).start()

    def drain(ref, count, which, side):
        at = ref.at[pl.ds(0, count)]
        pltpu.make_async_copy(at, at, dma.at[2 * which + side]).wait()

    def greet(p, r):
        pl.semaphore_signal(barrier, inc=1, device_id=(p, r), device_id_type=MESH)

    def in_group(i):
        return y * GROUP + (g + i) % GROUP

    def in_outer(i):
        return (y + i) % outer * GROUP + g

    loop(1, GROUP, lambda i: greet(in_group(i), rep))
    loop(1, outer, lambda i: greet(in_outer(i), rep))
    loop(1, reps, lambda i: greet(me, (rep + i) % reps))
    loads = [pltpu.make_async_copy(a, b, load.at[i]) for i, (a, b) in enumerate(
        [(owner_h, owner_v), (row_h, row_v), (table_h, table_v), (filt_h, filt_v), (relid_h, relid_v), (rel_h, rel_v),
         (projt_h, projt_v), (rare_h, rare_v)])]
    for copy in loads:
        copy.start()

    loads[0].wait()
    loads[1].wait()
    owner = owner_v[...]
    named = one(iota((ent, req), 0) == owner)
    before = one(iota((req, req), 0) < iota((req, req), 1))
    rank = jnp.sum(named.astype(F32) * mm(named, before), 0, keepdims=True).astype(I32)
    slot = rank * ent + owner
    spot = owner % GROUP * (outer * CAP) + y * CAP + rank
    wide = GROUP * outer * CAP
    high, low = split(jnp.where(iota((wide, req), 0) == spot, row_v[...].reshape(1, req).astype(F32), 0.0))
    heard = one(iota((outer, req), 0) == owner // GROUP)
    ids = mm(heard, high, NT) + mm(heard, low, NT)
    for j in range(wide // 128):
        send1[:, j, :] = ids[:, j * 128 : (j + 1) * 128]
    got1[pl.ds(y, 1)] = send1[pl.ds(y, 1)]
    pl.semaphore_wait(barrier, GROUP + outer + reps - 3)
    loop(1, outer, lambda i: remote(send1.at[(y + i) % outer], got1.at[y], 0, in_outer(i), rep))
    loads[2].wait()
    table_high, table_low = split(table_v[...])
    drain(got1, outer - 1, 0, 1)
    send2[...] = jnp.sum(got1[...], 0).reshape(wide // 128, 1, 128)
    share = GROUP * 128 // wide
    got2[pl.ds(g, 1)] = send2[pl.ds(g // share, 1)]
    loop(1, GROUP, lambda i: remote(send2.at[(g + i) % GROUP // share], got2.at[g], 1, in_group(i), rep))
    drain(got2, GROUP - 1, 1, 1)
    src = iota((slots, GROUP), 0) % ent
    pick = one(src % GROUP == iota((slots, GROUP), 1))
    high, low = split(got2[...].reshape(GROUP, 128))
    spread = mm(pick, high) + mm(pick, low)
    at = iota((slots, 128), 0)
    keep = g % share * (outer * CAP) + at % ent // GROUP * CAP + at // ent == iota((slots, 128), 1)
    wanted = jnp.sum(jnp.where(keep, spread, 0.0), 1, keepdims=True)
    hot_rows = one(iota((slots, rows), 1).astype(F32) == wanted)
    picked = mm(hot_rows, table_high[:128], NT) + mm(hot_rows, table_low[:128], NT)
    for j in range(CAP):
        found[:, j, :] = picked[j * ent : (j + 1) * ent]
    loop(1, ent, lambda i: remote(found.at[(me + i) % ent], fetched.at[me], 2, (me + i) % ent, rep))
    blank = jnp.zeros((128 - tail, rows), BF16)
    picked = (mm(hot_rows, jnp.concatenate([table_high[128:], blank], 0), NT)
              + mm(hot_rows, jnp.concatenate([table_low[128:], blank], 0), NT))
    for j, piece_of in enumerate(pack_tail(picked, ent, tail)):
        found_b[:, j, :] = piece_of
    loop(1, ent, lambda i: remote(found_b.at[(me + i) % ent], fetched_b.at[me], 16, (me + i) % ent, rep))
    fetched[pl.ds(me, 1)] = found[pl.ds(me, 1)]
    fetched_b[pl.ds(me, 1)] = found_b[pl.ds(me, 1)]

    loads[3].wait()
    band = band_matrix(filt_v[...].T)
    band_high, band_low = split(band)
    lhs_v[...] = jnp.concatenate([band_high, band_high, band_low], 1)
    bandt_v[...] = jnp.concatenate([band, band - band_high.astype(F32)], 1).T.astype(BF16)
    loads[4].wait()
    loads[5].wait()
    img[...] = jnp.zeros(img.shape, F32)
    strip[...] = mm(rel_v[...], one(iota((rels, batch), 0) == relid_v[...].reshape(1, batch)))
    fill_image(img, HEAD_ROWS, strip, HEAD_ROWS)
    loads[6].wait()

    def turn_over(i, c):
        at = pl.ds(pl.multiple_of(i * 512, 512), 512)
        proj_v[at, :] = projt_v[:, at].T
        return c

    lax.fori_loop(0, FILT * PER // 512, turn_over, 0)
    rel_at = pl.ds(HEAD_ROWS * PITCH, HEAD_ROWS * PITCH)
    hi_img[rel_at, :] = img[rel_at, :].astype(BF16)
    lo_img[rel_at, :] = jnp.zeros((HEAD_ROWS * PITCH, batch), BF16)

    def conv(q):
        at = pl.ds(pl.multiple_of(q * 2 * PITCH, 2 * PITCH), 4 * PITCH)
        hi, lo = hi_img[at, :], lo_img[at, :]
        v = mm(lhs_v[...], jnp.concatenate([hi, lo, hi], 0))
        s = sigmoid(v)
        a = v * s
        out = pl.ds(pl.multiple_of(q * 16, 16), 16)
        feat[:, out, :] = a.astype(BF16).reshape(FILT, 16, batch)
        dact[:, out, :] = (s + a * (1.0 - s)).reshape(FILT, 16, batch)

    def conv_two(q):
        def stack(k):
            at = pl.ds(k * 2 * PITCH, 4 * PITCH)
            hi, lo = hi_img[at, :], lo_img[at, :]
            return jnp.concatenate([hi, lo, hi], 0)

        v = mm(lhs_v[...], jnp.concatenate([stack(q), stack(q + 1)], 1))
        s = sigmoid(v)
        a = v * s
        d = s + a * (1.0 - s)
        for k in range(2):
            out, lanes = pl.ds((q + k) * 16, 16), slice(k * batch, (k + 1) * batch)
            feat[:, out, :] = a[:, lanes].astype(BF16).reshape(FILT, 16, batch)
            dact[:, out, :] = d[:, lanes].reshape(FILT, 16, batch)

    loop(HEAD_PAIRS, PAIRS, conv)
    drain(fetched, ent - 1, 2, 1)

    hot = one(iota((slots, req), 0) == slot)
    high, low = split(jnp.concatenate([fetched[:, j, :] for j in range(CAP)], 0))
    val[pl.ds(0, 128), :] = mm(high, hot, TN) + mm(low, hot, TN)
    full = 128 // IMG_COLS
    early = (full - 2) // 4 * 2
    strip[pl.ds(0, 128), :] = val[pl.ds(0, 128), pl.ds(0, batch)]

    def take_rows(first, last):
        for r in range(first, last):
            img[pl.ds(PITCH * r, IMG_COLS), :] = strip[pl.ds(IMG_COLS * r, IMG_COLS), :]
        at = pl.ds(PITCH * first, PITCH * (last - first))
        high, low = split(img[at, :])
        hi_img[at, :] = high
        lo_img[at, :] = low

    take_rows(0, full)
    for q in range(0, early, 2):
        conv_two(q)
    drain(fetched_b, ent - 1, 16, 1)
    high, low = split(unpack_tail(fetched_b[:, 0, :], fetched_b[:, 1, :], fetched_b[:, 2, :], tail))
    val[pl.ds(128, tail), :] = (mm(high, hot, TN) + mm(low, hot, TN))[:tail]
    strip[pl.ds(128, tail), :] = val[pl.ds(128, tail), pl.ds(0, batch)]
    take_rows(full, HEAD_ROWS)
    for q in range(early, HEAD_PAIRS, 2):
        conv_two(q)
    projected = mm(projt_v[...], feat[...].reshape(FILT * PER, batch))
    sig = sigmoid(projected)
    hidden = projected * sig
    pos, negs = val[:, pl.ds(batch, batch)], val[:, pl.ds(2 * batch, neg)]
    score_pos = jnp.sum(hidden * pos, 0, keepdims=True)
    score_neg = mm_hi(negs, hidden, TN)
    grad_pos = -sigmoid(-score_pos)
    grad_neg = sigmoid(score_neg) / neg
    grad_hidden = grad_pos * pos + mm_hi(negs, grad_neg)
    grad_proj = (grad_hidden * sig * (1.0 + projected * (1.0 - sig))).astype(BF16)
    val[:, pl.ds(batch, batch)] = grad_pos * hidden
    val[:, pl.ds(2 * batch, neg)] = mm_hi(hidden, grad_neg, NT)
    dimg[...] = jnp.zeros(dimg.shape, F32)

    def back(q):
        out = pl.ds(pl.multiple_of(q * 16, 16), 16)
        turned = proj_v.reshape(FILT, PER, width)[:, out, :].reshape(BAND, width)
        d = mm(turned, grad_proj) * dact[:, out, :].reshape(BAND, batch)
        return split(d)

    def head_back(first, last):
        for q in range(first, last):
            left = jnp.concatenate(back(q), 1)
            left_v[q] = left
            both = mm(bandt_v[...], left)
            at = pl.ds(q * 2 * PITCH, 4 * PITCH)
            dimg[at, :] += both[:64, :batch] + both[64:, :batch] + both[:64, batch:]

    def head_rows(first, last):
        for r in range(first, last):
            strip[pl.ds(IMG_COLS * r, IMG_COLS), :] = dimg[pl.ds(PITCH * r, IMG_COLS), :]

    cut_pair = (128 // IMG_COLS + 2) // 2
    cut_row = 128 // IMG_COLS + 1
    head_back(0, cut_pair)
    head_rows(0, cut_row)
    val[pl.ds(0, 128), pl.ds(0, batch)] = strip[pl.ds(0, 128), :]
    high, low = split(val[pl.ds(0, 128), :])
    packed = mm(hot, high, NT) + mm(hot, low, NT)
    for j in range(CAP):
        out_a[:, j, :] = packed[j * ent : (j + 1) * ent]
    loop(1, ent, lambda i: remote(out_a.at[(me + i) % ent], land_a.at[me], 3, (me + i) % ent, rep))
    head_back(cut_pair, HEAD_PAIRS)
    head_rows(cut_row, HEAD_ROWS)
    val[pl.ds(128, tail), pl.ds(0, batch)] = strip[pl.ds(128, tail), :]
    high, low = split(val[pl.ds(128, tail), :])
    blank = jnp.zeros((128 - tail, req), BF16)
    packed = (mm(hot, jnp.concatenate([high, blank], 0), NT) + mm(hot, jnp.concatenate([low, blank], 0), NT))
    for j, piece_of in enumerate(pack_tail(packed, ent, tail)):
        out_b[:, j, :] = piece_of
    loop(1, ent, lambda i: remote(out_b.at[(me + i) % ent], land_b.at[me], 11, (me + i) % ent, rep))
    land_a[pl.ds(me, 1)] = out_a[pl.ds(me, 1)]
    land_b[pl.ds(me, 1)] = out_b[pl.ds(me, 1)]

    acc_v[...] = jnp.zeros(acc_v.shape, F32)

    def add_filter(q, left):
        at = pl.ds(pl.multiple_of(q * 2 * PITCH, 2 * PITCH), 4 * PITCH)
        hi, lo = hi_img[at, :], lo_img[at, :]
        right = jnp.concatenate([jnp.concatenate([hi, hi], 1), jnp.concatenate([lo, jnp.zeros_like(lo)], 1)], 0)
        acc_v[...] += mm(left, right, NT)

    loop(0, HEAD_PAIRS, lambda q: add_filter(q, left_v[q]))
    loop(HEAD_PAIRS, PAIRS, lambda q: add_filter(q, jnp.concatenate(back(q), 1)))
    both = acc_v[...]
    acc_v[...] = both + pltpu.roll(both, 64, 1)
    taps = acc_v[pl.ds(0, FILT, stride=16), :]
    for k in range(1, 16):
        shift = k // OUT_COLS * PITCH + k % OUT_COLS
        taps = taps + pltpu.roll(acc_v[pl.ds(k, FILT, stride=16), :], 128 - shift, 1)
    turn[...] = jnp.concatenate([taps, jnp.zeros((128 - FILT, 128), F32)], 0).T
    filter_part = jnp.concatenate(
        [sum(pltpu.roll(turn[pl.ds(PITCH * i + j, 1), :], FILT * j, 1) for j in range(3)) for i in range(3)], 0)
    f_here[0] = filter_part
    f_x[pl.ds(rep, 1)] = filter_part[None]
    loop(1, reps, lambda i: remote(f_here.at[0], f_x.at[rep], 5, me, (rep + i) % reps))
    drain(land_a, ent - 1, 3, 1)

    def share_out(sums, here, there, which):
        for r in range(reps):
            here[r] = sums[:, r * piece : (r + 1) * piece]
        there[pl.ds(rep, 1)] = here[pl.ds(rep, 1)]
        loop(1, reps, lambda i: remote(here.at[(rep + i) % reps], there.at[rep], which, me, (rep + i) % reps))

    def columns(r):
        return pl.ds(pl.multiple_of(r * piece, piece), piece)

    high, low = split(jnp.concatenate([land_a[:, j, :] for j in range(CAP)], 0))
    share_out(mm(high, hot_rows, TN) + mm(low, hot_rows, TN), part_a, pland_a, 4)
    drain(land_b, ent - 1, 11, 1)
    high, low = split(unpack_tail(land_b[:, 0, :], land_b[:, 1, :], land_b[:, 2, :], tail))
    share_out((mm(high, hot_rows, TN) + mm(low, hot_rows, TN))[:tail], part_b, pland_b, 12)
    drain(f_x, reps - 1, 5, 1)
    f_here[1] = jnp.sum(f_x[...], 0)
    f_g[pl.ds(g, 1)] = f_here[pl.ds(1, 1)]
    loop(1, GROUP, lambda i: remote(f_here.at[1], f_g.at[g], 6, in_group(i), rep))
    drain(pland_a, reps - 1, 4, 1)
    drain(pland_b, reps - 1, 12, 1)
    block = table_v[:, columns(rep)] - learn_rate * jnp.concatenate([jnp.sum(pland_a[...], 0), jnp.sum(pland_b[...], 0)], 0)
    n_here[0] = jnp.sqrt(jnp.sum(block * block, 0, keepdims=True) + norm_eps)
    upd[:, columns(rep)] = block
    n_a[pl.ds(rep * outer + y, 1)] = n_here[pl.ds(0, 1)]
    loop(1, reps * outer, lambda i: remote(n_here.at[0], n_a.at[rep * outer + y], 9, in_outer(i), (rep + i // outer) % reps))
    right, left = (rep + 1) % reps, (rep + reps - 1) % reps
    upper, lower = pl.ds(0, half), pl.ds(half, width - half)

    def pass_on(at, r, which, to):
        remote(upd.at[at, columns(r)], upd.at[at, columns(r)], which, me, to)

    def arrived(at, r, which, side):
        ref = upd.at[at, columns(r)]
        pltpu.make_async_copy(ref, ref, dma.at[2 * which + side]).wait()

    everything = pl.ds(0, width)
    pass_on(everything, rep, 8, right)
    pass_on(everything, rep, 13, left)
    drain(f_g, GROUP - 1, 6, 1)
    f_here[2] = jnp.sum(f_g[...], 0)
    f_y[pl.ds(y, 1)] = f_here[pl.ds(2, 1)]
    loop(1, outer, lambda i: remote(f_here.at[2], f_y.at[y], 7, in_outer(i), rep))
    drain(n_a, reps * outer - 1, 9, 1)
    n_here[1] = jnp.sum(n_a[...], 0)
    n_b[pl.ds(g, 1)] = n_here[pl.ds(1, 1)]
    loop(1, GROUP, lambda i: remote(n_here.at[1], n_b.at[g], 10, in_group(i), rep))
    arrived(everything, left, 8, 1)
    pass_on(upper, left, 14, right)
    arrived(everything, right, 13, 1)
    pass_on(lower, right, 15, left)
    far = (rep + 2) % reps
    arrived(upper, far, 14, 1)
    arrived(lower, far, 15, 1)
    updated = upd[...]
    norm = jnp.sqrt(jnp.sum(updated * updated, 0, keepdims=True) + norm_eps)
    loads[7].wait()
    drain(f_y, outer - 1, 7, 1)
    total_ref[...] = jnp.sum(f_y[...], 0)
    drain(send1, outer - 1, 0, 0)
    drain(got2, GROUP - 1, 1, 0)
    drain(found, ent - 1, 2, 0)
    drain(found_b, ent - 1, 16, 0)
    drain(out_a, ent - 1, 3, 0)
    drain(out_b, ent - 1, 11, 0)
    drain(part_a, reps - 1, 4, 0)
    drain(part_b, reps - 1, 12, 0)
    drain(f_x, reps - 1, 5, 0)
    drain(f_g, GROUP - 1, 6, 0)
    drain(f_y, outer - 1, 7, 0)
    arrived(everything, rep, 8, 0)
    arrived(everything, rep, 13, 0)
    arrived(upper, left, 14, 0)
    arrived(lower, right, 15, 0)
    drain(n_a, reps * outer - 1, 9, 0)
    drain(n_b, GROUP - 1, 10, 1)
    drain(n_b, GROUP - 1, 10, 0)
    norm_total = jnp.sum(jnp.sum(n_b[...], 0), 1, keepdims=True)
    target = 0.25 * run_ref[...] + 0.75 * norm_total / (rows * ent)
    out_ref[...] = updated * jnp.where(rare_v[...].reshape(1, rows) == 1, target / norm, 1.0)


def step(owner, row, relid, rare, run, table_t, rel_t, filt, proj_t, ent, reps):
    width, rows = table_t.shape
    req, batch, feats = owner.shape[1], relid.shape[0], proj_t.shape[1]
    piece, outer = rows // reps, ent // GROUP
    vmem, hbm = pl.BlockSpec(memory_space=pltpu.VMEM), pl.BlockSpec(memory_space=pltpu.HBM)
    v = pltpu.VMEM
    wide = GROUP * outer * CAP
    first, second = v((ent, CAP, 128), F32), v((ent, 3, 128), F32)
    return pl.pallas_call(
        functools.partial(step_kernel, ent, reps),
        out_shape=(jax.ShapeDtypeStruct((width, rows), F32), jax.ShapeDtypeStruct((3, 128), F32)),
        in_specs=[hbm] * 4 + [vmem] + [hbm] * 4, out_specs=(vmem,) * 2,
        scratch_shapes=[
            v(owner.shape, I32), v(row.shape, I32), v(relid.shape, I32), v(rare.shape, I32), v((width, rows), F32),
            v(rel_t.shape, BF16), v(filt.shape, F32), v(proj_t.shape, BF16),
            v((feats, width), BF16), v((outer, wide // 128, 128), F32), v((outer, wide // 128, 128), F32),
            v((wide // 128, 1, 128), F32), v((GROUP, 1, 128), F32), first, second, first, second, first, second, first, second,
            v((width, req), F32), v((width, batch), F32), v((IMG_ROWS * PITCH, batch), F32),
            v((IMG_ROWS * PITCH, batch), BF16), v((IMG_ROWS * PITCH, batch), BF16), v((BAND, 192), BF16),
            v((128, BAND), BF16), v((FILT, PER, batch), BF16), v((FILT, PER, batch), F32),
            v((HEAD_PAIRS, BAND, 2 * batch), BF16), v(((HEAD_ROWS + 2) * PITCH, batch), F32), v((BAND, 128), F32),
            v((128, 128), F32),
            v((reps, 128, piece), F32), v((reps, width - 128, piece), F32),
            v((reps, 128, piece), F32), v((reps, width - 128, piece), F32), v((width, rows), F32), v((3, 3, 128), F32),
            v((reps, 3, 128), F32), v((GROUP, 3, 128), F32), v((outer, 3, 128), F32),
            v((2, 1, 128), F32), v((reps * outer, 1, 128), F32), v((GROUP, 1, 128), F32),
            pltpu.SemaphoreType.DMA((8,)), pltpu.SemaphoreType.DMA((34,))],
        compiler_params=pltpu.CompilerParams(collective_id=0, has_side_effects=True, vmem_limit_bytes=44 << 20),
        name="step",
    )(*[pltpu.with_memory_space_constraint(a, pltpu.HBM) for a in (owner, row, relid, rare)], run, *[pltpu.with_memory_space_constraint(a, pltpu.HBM) for a in (table_t, rel_t, filt, proj_t)])


def body(entity_table, relation_table, filters, projection, request_owner, request_row, relation_id, rare_flag, running_norm):
    ent, reps = lax.axis_size("ent"), lax.axis_size("rep")
    batch, req = relation_id.shape[0], request_row.shape[0]
    new_t, total = step(request_owner.reshape(1, req), request_row, relation_id, rare_flag, running_norm.reshape(1, 1),
                        entity_table.T, relation_table.T, filters.T, projection.T, ent, reps)
    filter_grad = total[:, : 3 * FILT].reshape(9, FILT).T / (batch * ent * reps)
    return new_t.T, filter_grad


def solution(mesh):
    in_specs = (P("ent", None), P(), P(), P(), P(("ent", "rep"), None), P(("ent", "rep")), P(("ent", "rep")), P("ent"), P())
    return jax.shard_map(body, mesh=mesh, in_specs=in_specs, out_specs=(P("ent", None), P()), check_vma=False)
```
